32 devices in a mesh: dp: 8 (over z, x), tensor: 4 (over y, core).
Axes of the slice: x: 2, y: 2, z: 4, core: 2. Of those that a mesh axis runs over, the one named last changes fastest.
Arguments:
- prefix: bfloat16 [8, 128, 8192], P('dp'), may hold values from -6 to 6
- kv_weight: bfloat16 [8192, 2, 512], P(None, None, 'tensor'), may hold values from -0.044194174 to 0.044194174
- ans_query: bfloat16 [8192, 4096], P('dp', 'tensor'), may hold values from -60 to 60
- ans_kv: bfloat16 [8192, 2, 512], P('dp', None, 'tensor'), may hold values from -8 to 8
- d_out: bfloat16 [8192, 4096], P('dp', 'tensor'), may hold values from -192 to 192
- branch_prompt: int32 [16], P('dp'), may hold values from 0 to 7, as said below
Outputs:
- attn_out: bfloat16 [8192, 4096], P('dp', 'tensor')
- prefix_grad: bfloat16 [8, 128, 8192], P('dp', 'tensor')
The draws below stay inside these ranges and needn't reach their ends.
Inputs may be any that keep to these rules, and one draw needn't show every extreme that they name: `branch_prompt`: prompt p is owned by dp index p. The dp index that holds a branch and the owner of its prompt are at most 3 steps apart, counting around the axis. Every dp index holds at least one answer to its own prompt.
All inputs are finite; a program needn't handle non-finite values.
Results may differ from the reference program's by a relative error of at most 0.014.
The reference program's roundings to bfloat16 on the way count: a program that leaves them out, or rounds other values in their place, can miss the bound.
Values may be sent and summed in bfloat16 or wider, within the bound.
No kernel may reach another device: no remote copies, remote signals or barrier semaphores. Data moves between devices by JAX's collectives and lax.ppermute only.
A program may use at most 128 MiB of HBM per device.

```python
import math
import jax
import jax.numpy as jnp
from jax import lax

D = 8192
QH = 32
KVH = 4
HD = 128
PFX = 128
ANS = 512
BR_DEV = 2
REACH = 3
PROMPTS = 8
BRANCHES = 16
TOKENS = 8192


def weight_draw(key):
    normal_part = jax.random.truncated_normal(jax.random.fold_in(key, 31), -4.0, 4.0, (D, 2, KVH * HD), jnp.float32)
    return normal_part * (1.0 / math.sqrt(D))


def draw_kv_weight(key, part):
    return weight_draw(key).astype(jnp.bfloat16)


def draw_prefix(key, part):
    values = jax.random.truncated_normal(jax.random.fold_in(key, 43), -6.0, 6.0, (PROMPTS, PFX, D), jnp.float32)
    return values.astype(jnp.bfloat16)


def answer_pair(key):
    groups = QH // KVH
    queries = jax.random.truncated_normal(jax.random.fold_in(key, 21), -6.0, 6.0, (BRANCHES, ANS, KVH, groups, HD), jnp.float32)
    key_rows = jax.random.truncated_normal(jax.random.fold_in(key, 22), -6.0, 6.0, (BRANCHES, ANS, KVH, HD), jnp.float32)
    value_rows = jax.random.truncated_normal(jax.random.fold_in(key, 23), -6.0, 6.0, (BRANCHES, ANS, KVH, HD), jnp.float32)
    return (queries, key_rows, value_rows)


def draw_ans_query(key, part):
    queries, key_rows, value_rows = answer_pair(key)
    return queries.reshape(TOKENS, QH * HD).astype(jnp.bfloat16)


def draw_ans_kv(key, part):
    queries, key_rows, value_rows = answer_pair(key)
    return jnp.stack([key_rows, value_rows], axis=2).reshape(TOKENS, 2, KVH * HD).astype(jnp.bfloat16)


def draw_branch_prompt(key, part):
    devices = jnp.arange(PROMPTS)
    offsets = jax.random.randint(jax.random.fold_in(key, 11), (PROMPTS, BR_DEV), -REACH, REACH + 1)
    own_slot = jax.random.randint(jax.random.fold_in(key, 12), (PROMPTS,), 0, BR_DEV)
    shuffled = jax.random.permutation(jax.random.fold_in(key, 13), PROMPTS)
    listed = jnp.arange(2 * REACH)
    listed = jnp.where(listed < REACH, listed - REACH, listed - REACH + 1)
    forced = jnp.zeros((PROMPTS,), jnp.int32).at[shuffled[:2 * REACH]].set(listed.astype(jnp.int32))
    has_forced = jnp.zeros((PROMPTS,), jnp.int32).at[shuffled[:2 * REACH]].set(1)
    slot_ids = jnp.arange(BR_DEV)
    second_slot = (own_slot + 1) % BR_DEV
    forced_here = (slot_ids[None, :] == second_slot[:, None]) & (has_forced[:, None] == 1)
    offsets = jnp.where(forced_here, forced[:, None], offsets)
    offsets = jnp.where(slot_ids[None, :] == own_slot[:, None], 0, offsets)
    return ((devices[:, None] + offsets) % PROMPTS).reshape(BRANCHES).astype(jnp.int32)


def steps_of(key, shape, shards, low, high):
    loudness, own = 1.0, jax.random.fold_in(key, 6)
    for axis_at, shards_of in shards:
        heights = jnp.exp(jax.random.uniform(jax.random.fold_in(own, axis_at), (shards_of,), jnp.float32, low / len(shards), high / len(shards)))
        loudness = loudness * jnp.repeat(heights, shape[axis_at] // shards_of).reshape([-1 if axis == axis_at else 1 for axis in range(len(shape))])
    return loudness


def gaussian(own_key, extent, scale, bound, split=(), dtype=jnp.bfloat16):
    loudness = steps_of(own_key, extent, split, -0.22, 0.18) if split else 1.0
    entries = jax.random.normal(own_key, extent, jnp.float32) * scale * loudness
    return jnp.minimum(jnp.maximum(entries, -bound), bound).astype(dtype)


def setup_inputs(seed: int = 0) -> dict:
    key_list = jax.random.split(jax.random.key(seed), 7)
    prefix = draw_prefix(jax.random.fold_in(key_list[6], 71), 0)
    kv_weight = draw_kv_weight(jax.random.fold_in(key_list[6], 71), 0)
    ans_query = draw_ans_query(jax.random.fold_in(key_list[6], 71), 0)
    ans_kv = draw_ans_kv(jax.random.fold_in(key_list[6], 71), 0)
    d_out = gaussian(key_list[4], (TOKENS, QH * HD), 32.0, 192.0, ((0, 8), (1, 4)))
    branch_prompt = draw_branch_prompt(jax.random.fold_in(key_list[6], 71), 0)
    return dict(prefix=prefix, kv_weight=kv_weight, ans_query=ans_query, ans_kv=ans_kv, d_out=d_out, branch_prompt=branch_prompt)


def branch_pass(queries, key_rows, value_rows, upstream):
    answers = queries.shape[0]
    prefix_len = key_rows.shape[0] - answers
    scaling = queries.shape[-1] ** -0.5
    query_f = queries.astype(jnp.float32)
    key_f = key_rows.astype(jnp.float32)
    value_f = value_rows.astype(jnp.float32)
    upstream_f = upstream.astype(jnp.float32)
    scores = jnp.einsum("ahgd,khd->hgak", query_f, key_f) * scaling
    key_pos = jnp.arange(key_rows.shape[0])
    row_pos = jnp.arange(answers)
    allowed = (key_pos[None, :] < prefix_len) | (key_pos[None, :] - prefix_len <= row_pos[:, None])
    scores = jnp.where(allowed, scores, -jnp.inf)
    row_max = jnp.max(scores, axis=-1, keepdims=True)
    exps = jnp.exp(scores - row_max)
    prob_full = exps / jnp.sum(exps, axis=-1, keepdims=True)
    prob_half = lax.optimization_barrier(prob_full.astype(jnp.bfloat16)).astype(jnp.float32)
    context = jnp.einsum("hgak,khd->ahgd", prob_half, value_f)
    prob_grad = jnp.einsum("ahgd,khd->hgak", upstream_f, value_f)
    delta_row = jnp.einsum("ahgd,ahgd->hga", upstream_f, context)
    score_grad = prob_full * (prob_grad - delta_row[..., None])
    score_half = lax.optimization_barrier(score_grad.astype(jnp.bfloat16)).astype(jnp.float32)
    key_grad = jnp.einsum("hgak,ahgd->khd", score_half[..., :prefix_len], query_f) * scaling
    value_grad = jnp.einsum("hgak,ahgd->khd", prob_half[..., :prefix_len], upstream_f)
    return context.astype(jnp.bfloat16), key_grad, value_grad


def reference(prefix, kv_weight, ans_query, ans_kv, d_out, branch_prompt):
    groups = QH // KVH
    flat_weight = kv_weight.reshape(D, 2 * KVH * HD)

    def project(prompt_rows):
        return jnp.dot(prompt_rows, flat_weight, preferred_element_type=jnp.float32).astype(jnp.bfloat16)

    prompt_kv = lax.map(project, prefix).reshape(PROMPTS, PFX, 2, KVH, HD)
    queries = ans_query.reshape(BRANCHES, ANS, KVH, groups, HD)
    answer_kv = ans_kv.reshape(BRANCHES, ANS, 2, KVH, HD)
    upstream = d_out.reshape(BRANCHES, ANS, KVH, groups, HD)

    def one_branch(packed):
        branch_q, branch_kv, branch_up, prompt_id = packed
        own_kv = lax.dynamic_index_in_dim(prompt_kv, prompt_id.astype(jnp.int32), 0, keepdims=False)
        key_rows = jnp.concatenate([own_kv[:, 0], branch_kv[:, 0]], axis=0)
        value_rows = jnp.concatenate([own_kv[:, 1], branch_kv[:, 1]], axis=0)
        return branch_pass(branch_q, key_rows, value_rows, branch_up)

    context, key_grad, value_grad = lax.map(one_branch, (queries, answer_kv, upstream, branch_prompt))
    attn_out = context.reshape(TOKENS, QH * HD)
    both_grads = jnp.stack([key_grad, value_grad], axis=2).reshape(BRANCHES, PFX * 2 * KVH * HD)
    kv_sum = jax.ops.segment_sum(both_grads, branch_prompt, num_segments=PROMPTS)
    kv_grad = kv_sum.astype(jnp.bfloat16).reshape(PROMPTS, PFX, 2 * KVH * HD)

    def project_back(grad_rows):
        return lax.dot_general(grad_rows, flat_weight, (((1,), (1,)), ((), ())), preferred_element_type=jnp.float32).astype(jnp.bfloat16)

    prefix_grad = lax.map(project_back, kv_grad)
    return attn_out, prefix_grad
```

```python
import functools
import math

import jax
import jax.numpy as jnp
from jax import lax
from jax.experimental import pallas as pl
from jax.experimental.pallas import tpu as pltpu
from jax.sharding import PartitionSpec as P

HD = 128
REACH = 3
BLOCK = 128
HEADS_PER_STEP = 2
OWN, PARTNER, LOW, LOW_PAIR, HIGH, HIGH_PAIR, FAR, SOURCES = range(8)


def dp_permute(x, target):
    devices = lax.axis_size("dp")
    return lax.ppermute(x, "dp", [(i, target(i) % devices) for i in range(devices)])


def far_of(i):
    return i + REACH if i % 2 else i - REACH


def first_own(prompts, me, branches):
    own = jnp.int32(branches - 1)
    for slot in reversed(range(branches)):
        own = jnp.where(prompts[slot] == me, slot, own)
    return own


def branch_at(step, first, prompts, me, branches):
    own = first_own(prompts, me, branches)
    if first:
        return own
    return step + jnp.where(step >= own, 1, 0)


def source_of(prompt, me, devices):
    rel = lax.rem(prompt - me + devices, devices)
    rel = jnp.where(rel > REACH, rel - devices, rel)
    odd = lax.rem(me, 2) == 1
    source = jnp.where(rel == 0, OWN, FAR)
    source = jnp.where(rel == -2, LOW, source)
    source = jnp.where(rel == 2, HIGH, source)
    source = jnp.where(rel == 1, jnp.where(odd, HIGH_PAIR, PARTNER), source)
    source = jnp.where(rel == -1, jnp.where(odd, PARTNER, LOW_PAIR), source)
    source = jnp.where(rel == 3, jnp.where(odd, FAR, HIGH_PAIR), source)
    source = jnp.where(rel == -3, jnp.where(odd, LOW_PAIR, FAR), source)
    return source


def contract(a, b, dim_a, dim_b):
    return lax.dot_general(
        a, b, (((dim_a,), (dim_b,)), ((), ())), preferred_element_type=jnp.float32
    )


def one_head(q_ref, up_ref, out_ref, keys, values, half_grad, half_prob, head, answers, prefix_len):
    scale = HD**-0.5 * math.log2(math.e)
    cols = pl.ds(head * HD, HD)
    rows_at = lax.broadcasted_iota(jnp.int32, (BLOCK, BLOCK), 0)
    keys_at = lax.broadcasted_iota(jnp.int32, (BLOCK, BLOCK), 1)
    allowed = keys_at <= rows_at
    for block in range(answers // BLOCK):
        rows = pl.ds(block * BLOCK, BLOCK)
        seen = prefix_len + (block + 1) * BLOCK
        scores = contract(q_ref[rows, cols], keys[:seen, :], 1, 1)
        last = jnp.where(allowed, scores[:, seen - BLOCK :], -1e30)
        scores = jnp.concatenate([scores[:, : seen - BLOCK], last], axis=1)
        row_max = jnp.max(scores, axis=1, keepdims=True)
        exps = jnp.exp2((scores - row_max) * scale)
        probs = exps * (1.0 / jnp.sum(exps, axis=1, keepdims=True))
        prob_half = probs.astype(jnp.bfloat16)
        context = contract(prob_half, values[:seen, :], 1, 0)
        out_ref[rows, cols] = context.astype(jnp.bfloat16)
        upstream = up_ref[rows, cols]
        prob_grad = contract(upstream, values[:prefix_len, :], 1, 1)
        delta_row = jnp.sum(upstream.astype(jnp.float32) * context, axis=1, keepdims=True)
        score_grad = probs[:, :prefix_len] * (prob_grad - delta_row)
        half_grad[rows, :] = score_grad.astype(jnp.bfloat16)
        half_prob[rows, :] = prob_half[:, :prefix_len]
    key_grad = contract(half_grad[...], q_ref[:, cols], 0, 0)
    value_grad = contract(half_prob[...], up_ref[:, cols], 0, 0)
    return key_grad, value_grad


def attention_kernel(first, devices, branches, info, prompts, *refs):
    if first:
        own_ref, q_ref, k_ref, v_ref, up_ref, out_ref, own_grad = refs[:7]
        keys, values, half_grad, half_prob, grads = refs[7:]
    else:
        own_ref, partner_ref, low_ref, high_ref, far_ref = refs[:5]
        q_ref, k_ref, v_ref, up_ref, _, out_ref = refs[5:11]
        own_grad, partner_grad, low_grad, high_grad, far_grad = refs[11:16]
        keys, values, half_grad, half_prob, grads = refs[16:]
    prefix_len = own_ref.shape[0]
    answers = q_ref.shape[0]
    step, part = pl.program_id(0), pl.program_id(1)
    me = info[0]
    branch = branch_at(step, first, prompts, me, branches)
    source = jnp.int32(OWN) if first else source_of(prompts[branch], me, devices)

    @pl.when((step == 0) & (part == 0))
    def _():
        grads[...] = jnp.zeros_like(grads)

    @pl.when(part == 0)
    def _():
        def take(piece):
            keys[:prefix_len, :] = piece[:, :HD]
            values[:prefix_len, :] = piece[:, HD:]

        if first:
            take(own_ref[...])
        else:
            pieces = (
                own_ref,
                partner_ref,
                low_ref.at[0],
                low_ref.at[1],
                high_ref.at[0],
                high_ref.at[1],
                far_ref,
            )
            for number, piece in enumerate(pieces):

                @pl.when(source == number)
                def _(piece=piece):
                    take(piece[...])

        keys[prefix_len:, :] = k_ref[...]
        values[prefix_len:, :] = v_ref[...]

    for head in range(HEADS_PER_STEP):
        key_grad, value_grad = one_head(
            q_ref, up_ref, out_ref, keys, values, half_grad, half_prob, head, answers, prefix_len
        )
        grads[source, :, :HD] += key_grad
        grads[source, :, HD:] += value_grad

    @pl.when((step == pl.num_programs(0) - 1) & (part == pl.num_programs(1) - 1))
    def _():
        def total(number):
            return jnp.concatenate(
                [grads[number, :, :HD] * HD**-0.5, grads[number, :, HD:]], axis=1
            )

        own_grad[...] = total(OWN)
        if not first:
            partner_grad[...] = total(PARTNER).astype(jnp.bfloat16)
            low_grad[0] = total(LOW).astype(jnp.bfloat16)
            low_grad[1] = total(LOW_PAIR).astype(jnp.bfloat16)
            high_grad[0] = total(HIGH).astype(jnp.bfloat16)
            high_grad[1] = total(HIGH_PAIR).astype(jnp.bfloat16)
            far_grad[...] = total(FAR).astype(jnp.bfloat16)


def attention(first, devices, me, prompts, pieces, query, keys, values, upstream, out):
    branches = prompts.shape[0]
    answers = query.shape[0] // branches
    width = query.shape[1]
    prefix_len = pieces[0].shape[0]
    part_width = HEADS_PER_STEP * HD
    steps = 1 if first else branches - 1

    def at(step, part, info, prompts):
        return branch_at(step, first, prompts, info[0], branches)

    wide = pl.BlockSpec((answers, part_width), lambda s, p, i, b: (at(s, p, i, b), p))
    narrow = pl.BlockSpec((answers, HD), lambda s, p, i, b: (at(s, p, i, b), 0))

    def whole(shape):
        return pl.BlockSpec(shape, lambda s, p, i, b: (0,) * len(shape))

    piece = (prefix_len, 2 * HD)
    in_specs = [whole(x.shape) for x in pieces] + [wide, narrow, narrow, wide]
    operands = [*pieces, query, keys, values, upstream]
    out_shape = [
        jax.ShapeDtypeStruct(query.shape, query.dtype),
        jax.ShapeDtypeStruct(piece, jnp.float32),
    ]
    out_specs = [wide, whole(piece)]
    aliases = {}
    if not first:
        in_specs.append(pl.BlockSpec(memory_space=pl.ANY))
        aliases = {2 + len(operands): 0}
        operands.append(out)
        for shape in (piece, (2, *piece), (2, *piece), piece):
            out_shape.append(jax.ShapeDtypeStruct(shape, jnp.bfloat16))
            out_specs.append(whole(shape))
    seen = prefix_len + (answers + BLOCK) // 2
    work = steps * answers * width
    return pl.pallas_call(
        functools.partial(attention_kernel, first, devices, branches),
        grid_spec=pltpu.PrefetchScalarGridSpec(
            num_scalar_prefetch=2,
            grid=(steps, width // part_width),
            in_specs=in_specs,
            out_specs=out_specs,
            scratch_shapes=[
                pltpu.VMEM((prefix_len + answers, HD), jnp.bfloat16),
                pltpu.VMEM((prefix_len + answers, HD), jnp.bfloat16),
                pltpu.VMEM((answers, prefix_len), jnp.bfloat16),
                pltpu.VMEM((answers, prefix_len), jnp.bfloat16),
                pltpu.VMEM((1 if first else SOURCES, prefix_len, 2 * HD), jnp.float32),
            ],
        ),
        out_shape=out_shape,
        input_output_aliases=aliases,
        compiler_params=pltpu.CompilerParams(dimension_semantics=("arbitrary", "arbitrary")),
        cost_estimate=pl.CostEstimate(
            flops=work * (4 * seen + 6 * prefix_len),
            bytes_accessed=6 * work,
            transcendentals=work // HD * seen,
        ),
        name="first_branch" if first else "other_branches",
    )(me, prompts, *operands)


def shards(prefix, kv_weight, ans_query, ans_kv, d_out, branch_prompt):
    prefix_len = prefix.shape[1]
    model_width = prefix.shape[2]
    columns = kv_weight.shape[2]
    if columns != HD:
        raise ValueError("one kv head")
    devices = lax.axis_size("dp")
    if devices % 2 or devices < 2 * REACH + 1:
        raise ValueError("dp size")
    flat_weight = kv_weight.reshape(kv_weight.shape[0], 2 * columns)
    own_kv = jnp.dot(prefix[0], flat_weight, preferred_element_type=jnp.float32).astype(
        jnp.bfloat16
    )
    me = lax.axis_index("dp").astype(jnp.int32).reshape(1)
    far = dp_permute(own_kv, far_of)
    partner = dp_permute(own_kv, lambda i: i ^ 1)
    pair = jnp.stack([own_kv, partner])
    low = dp_permute(pair, lambda i: i + 2)
    high = dp_permute(pair, lambda i: i - 2)
    answer_keys = ans_kv[:, 0]
    answer_values = ans_kv[:, 1]
    branch = functools.partial(attention, devices=devices, me=me, prompts=branch_prompt)
    out, own_grad = branch(
        True,
        pieces=[own_kv],
        query=ans_query,
        keys=answer_keys,
        values=answer_values,
        upstream=d_out,
        out=None,
    )
    out, more_grad, to_partner, to_low, to_high, to_far = branch(
        False,
        pieces=[own_kv, partner, low, high, far],
        query=ans_query,
        keys=answer_keys,
        values=answer_values,
        upstream=d_out,
        out=out,
    )
    from_far = dp_permute(to_far, far_of)
    from_high = dp_permute(to_low, lambda i: i - 2)
    from_low = dp_permute(to_high, lambda i: i + 2)

    def wide(x):
        return x.astype(jnp.float32)

    partner_sum = (wide(to_partner) + wide(from_high[1]) + wide(from_low[1])).astype(jnp.bfloat16)
    from_partner = dp_permute(partner_sum, lambda i: i ^ 1)
    kv_sum = own_grad + more_grad + wide(from_far) + wide(from_high[0]) + wide(from_low[0])
    kv_grad = (kv_sum + wide(from_partner)).astype(jnp.bfloat16)
    shares = lax.dot_general(
        kv_grad, flat_weight, (((1,), (1,)), ((), ())), preferred_element_type=jnp.float32
    ).astype(jnp.bfloat16)
    rows = sum_over_tensor(shares)
    return (out, rows.reshape(1, *rows.shape))


def sum_over_tensor(shares):
    count = lax.axis_size("tensor")
    index = lax.axis_index("tensor")
    if count & (count - 1):
        raise ValueError("tensor size")
    levels = count.bit_length() - 1
    rows = shares.shape[0] // count
    held = shares.reshape(*([2] * levels), rows, shares.shape[1])
    for level in range(levels):
        bit = 1 << level
        axis = levels - 1 - level
        mine = (index >> level) & 1
        keep = lax.dynamic_index_in_dim(held, mine, axis, keepdims=False)
        give = lax.dynamic_index_in_dim(held, 1 - mine, axis, keepdims=False)
        got = lax.ppermute(give, "tensor", [(i, i ^ bit) for i in range(count)])
        held = (keep.astype(jnp.float32) + got.astype(jnp.float32)).astype(jnp.bfloat16)
    return held


def solution(mesh):
    return jax.shard_map(
        shards,
        mesh=mesh,
        in_specs=(
            P("dp", None, None),
            P(None, None, "tensor"),
            P("dp", "tensor"),
            P("dp", None, "tensor"),
            P("dp", "tensor"),
            P("dp"),
        ),
        out_specs=(P("dp", "tensor"), P("dp", "tensor", None)),
        check_vma=False,
    )
```

```python
import functools
import math

import jax
import jax.numpy as jnp
from jax import lax
from jax.experimental import pallas as pl
from jax.experimental.pallas import tpu as pltpu
from jax.sharding import PartitionSpec as P

HD = 128
REACH = 3
BLOCK = 128
ROWS = 128
TALL = 4
TILE = 32
CHUNKS = 4
VMEM = 24 << 20
NOTES = 16
OWN, PARTNER, LOW, LOW_PAIR, HIGH, HIGH_PAIR, FAR = range(7)


def dp_permute(x, target):
    devices = lax.axis_size("dp")
    return lax.ppermute(x, "dp", [(i, target(i) % devices) for i in range(devices)])


def far_of(i):
    return i + REACH if i % 2 else i - REACH


def first_own(prompts, me, branches):
    own = jnp.int32(branches - 1)
    for slot in reversed(range(branches)):
        own = jnp.where(prompts[slot] == me, slot, own)
    return own


def other_branch(step, prompts, me, branches):
    own = first_own(prompts, me, branches)
    return step + jnp.where(step >= own, 1, 0)


def source_of(prompt, me, devices):
    rel = lax.rem(prompt - me + devices, devices)
    rel = jnp.where(rel > REACH, rel - devices, rel)
    odd = lax.rem(me, 2) == 1
    source = jnp.where(rel == 0, OWN, FAR)
    source = jnp.where(rel == -2, LOW, source)
    source = jnp.where(rel == 2, HIGH, source)
    source = jnp.where(rel == 1, jnp.where(odd, HIGH_PAIR, PARTNER), source)
    source = jnp.where(rel == -1, jnp.where(odd, PARTNER, LOW_PAIR), source)
    source = jnp.where(rel == 3, jnp.where(odd, FAR, HIGH_PAIR), source)
    source = jnp.where(rel == -3, jnp.where(odd, LOW_PAIR, FAR), source)
    return source


def contract(a, b, dim_a, dim_b):
    return lax.dot_general(
        a, b, (((dim_a,), (dim_b,)), ((), ())), preferred_element_type=jnp.float32
    )


def split_pairs(pairs, wide):
    rows = pairs.shape[0] // 2
    wide[...] = pairs.astype(jnp.float32)
    return [wide[pl.ds(at, rows, stride=2), :].astype(jnp.bfloat16) for at in range(2)]


def load_split(chunk, pairs, wide, split):
    size = wide.shape[1]
    keys, values = split_pairs(pairs[chunk * size : (chunk + 1) * size, :], wide.at[chunk % 2])
    split[chunk % 2, :, :HD] = keys
    split[chunk % 2, :, HD:] = values


def project_kernel(info, prompts, prefix_ref, weight_ref, out_ref, rows, pairs, wide, split, sems):
    depth = rows.shape[1] // CHUNKS
    copies = []
    for chunk in range(CHUNKS):
        deep = pl.ds(chunk * depth, depth)
        both = pl.ds(chunk * 2 * depth, 2 * depth)
        copies.append(
            (
                pltpu.make_async_copy(weight_ref.at[both, :], pairs.at[both, :], sems.at[0, chunk]),
                pltpu.make_async_copy(prefix_ref.at[:, deep], rows.at[:, deep], sems.at[1, chunk]),
            )
        )
    for pair in copies:
        for copy in pair:
            copy.start()
    total = jnp.zeros((rows.shape[0], out_ref.shape[1]), jnp.float32)
    for chunk in range(CHUNKS + 1):
        if chunk < CHUNKS:
            for copy in copies[chunk]:
                copy.wait()
            load_split(chunk, pairs, wide, split)
        if chunk:
            part = rows[:, (chunk - 1) * depth : chunk * depth]
            total += contract(part, split[(chunk - 1) % 2], 1, 0)
    out_ref[: rows.shape[0], :] = total.astype(out_ref.dtype)
    at = lax.broadcasted_iota(jnp.int32, (NOTES, out_ref.shape[1]), 0)
    notes = jnp.zeros(at.shape, jnp.float32)
    branches = prompts.shape[0]
    own = first_own(prompts, info[0], branches)
    for number in range(branches - 1):
        prompt = jnp.where(number >= own, prompts[number + 1], prompts[number])
        notes = jnp.where(at == number, prompt.astype(jnp.float32), notes)
    out_ref[rows.shape[0] :, :] = notes.astype(out_ref.dtype)


def project(me, prompts, prefix, kv_weight):
    prefix_len, model_width = prefix.shape
    there = pl.BlockSpec(memory_space=pl.ANY)
    return pl.pallas_call(
        project_kernel,
        in_specs=[pl.BlockSpec(memory_space=pltpu.SMEM)] * 2 + [there, there],
        out_specs=pl.BlockSpec(memory_space=pltpu.VMEM),
        out_shape=jax.ShapeDtypeStruct((prefix_len + NOTES, 2 * HD), jnp.bfloat16),
        scratch_shapes=[
            pltpu.VMEM(prefix.shape, jnp.bfloat16),
            pltpu.VMEM((2 * model_width, HD), jnp.bfloat16),
            pltpu.VMEM((2, 2 * model_width // CHUNKS, HD), jnp.float32),
            pltpu.VMEM((2, model_width // CHUNKS, 2 * HD), jnp.bfloat16),
            pltpu.SemaphoreType.DMA((2, CHUNKS)),
        ],
        cost_estimate=pl.CostEstimate(
            flops=4 * prefix_len * model_width * HD,
            bytes_accessed=2 * model_width * (prefix_len + 2 * HD),
            transcendentals=0,
        ),
        name="project",
    )(me, prompts, prefix, kv_weight.reshape(2 * model_width, HD))


def back_kernel(index, *refs):
    *grads, weight_ref, far_give, far_keep, near_give, near_keep, wide, split = refs
    depth = far_give.shape[1] // CHUNKS
    rows = far_give.shape[0]
    half, side = index[0] >> 1, index[0] & 1
    owners = (
        2 * (1 - half) + 1 - side,
        2 * (1 - half) + side,
        2 * half + 1 - side,
        2 * half + side,
    )
    parts = []
    for owner in owners:
        at = pl.ds(pl.multiple_of(owner * rows, rows), rows)
        total = grads[0][at, :].astype(jnp.float32)
        for grad in grads[1:]:
            total = total + grad[at, :].astype(jnp.float32)
        parts.append(total.astype(jnp.bfloat16))
    kv_grad = jnp.concatenate(parts, axis=0)
    for chunk in range(CHUNKS + 1):
        if chunk < CHUNKS:
            load_split(chunk, weight_ref, wide, split)
        if chunk:
            share = contract(kv_grad, split[(chunk - 1) % 2], 1, 1).astype(jnp.bfloat16)
            cols = pl.ds((chunk - 1) * depth, depth)
            for number, out in enumerate((far_give, far_keep, near_give, near_keep)):
                out[:, cols] = share[number * rows : (number + 1) * rows]


def back_shares(index, grads, kv_weight, count):
    model_width = kv_weight.shape[0]
    rows = grads[0].shape[0] // count
    here = pl.BlockSpec(memory_space=pltpu.VMEM)
    return pl.pallas_call(
        back_kernel,
        in_specs=[pl.BlockSpec(memory_space=pltpu.SMEM)]
        + [here] * (len(grads) + 1),
        out_specs=[here] * 4,
        out_shape=[jax.ShapeDtypeStruct((rows, model_width), jnp.bfloat16)] * 4,
        scratch_shapes=[
            pltpu.VMEM((2, 2 * model_width // CHUNKS, HD), jnp.float32),
            pltpu.VMEM((2, model_width // CHUNKS, 2 * HD), jnp.bfloat16),
        ],
        compiler_params=pltpu.CompilerParams(vmem_limit_bytes=VMEM),
        cost_estimate=pl.CostEstimate(
            flops=4 * grads[0].shape[0] * model_width * HD,
            bytes_accessed=2 * model_width * (grads[0].shape[0] + 2 * HD),
            transcendentals=0,
        ),
        name="back_shares",
    )(index, *grads, kv_weight.reshape(2 * model_width, HD))


def head_pass(heads, base, q_ref, up_ref, out_ref, keys, values, scratch, prefix_len):
    answers = keys.shape[0] - prefix_len
    scale = HD**-0.5 * math.log2(math.e)
    units = [(at, block) for at in range(0, len(heads), TALL) for block in range(answers // ROWS)]
    scores_at, probs_at, lead_at, half_grad, half_prob = scratch
    tall_rows = min(TALL, len(heads)) * ROWS

    def place(unit):
        at, block = units[unit]
        mine = range(at, min(at + TALL, len(heads)))
        return mine, block * ROWS, prefix_len + (block + 1) * ROWS

    def tall(ref, unit):
        mine, start, _ = place(unit)
        rows = pl.ds(pl.multiple_of(base + start, ROWS), ROWS)
        return jnp.concatenate(
            [ref[rows, heads[at] * HD : (heads[at] + 1) * HD] for at in mine], axis=0
        )

    def score(unit):
        seen = place(unit)[2]
        scores_at[unit % 2, :, :seen] = contract(tall(q_ref, unit), keys[:seen, :], 1, 1)

    def soften(unit):
        slot = unit % 2
        seen = place(unit)[2]
        for tile in range(tall_rows // TILE):
            rows = pl.ds(tile * TILE, TILE)
            first = tile * TILE % ROWS
            edge = seen - ROWS + first // BLOCK * BLOCK
            scores = scores_at[slot, rows, : edge + BLOCK]
            rows_at = lax.broadcasted_iota(jnp.int32, (TILE, BLOCK), 0) + first % BLOCK
            keys_at = lax.broadcasted_iota(jnp.int32, (TILE, BLOCK), 1)
            last = jnp.where(keys_at <= rows_at, scores[:, edge:], -jnp.inf)
            scores = jnp.concatenate([scores[:, :edge], last], axis=1)
            row_max = jnp.max(scores, axis=1, keepdims=True)
            exps = jnp.exp2((scores - row_max) * scale)
            probs = exps * (1.0 / jnp.sum(exps, axis=1, keepdims=True))
            lead_at[slot, rows, :] = probs[:, :prefix_len]
            probs_at[slot, rows, : edge + BLOCK] = probs.astype(jnp.bfloat16)
            if edge + BLOCK < seen:
                probs_at[slot, rows, edge + BLOCK : seen] = jnp.zeros(
                    (TILE, seen - edge - BLOCK), jnp.bfloat16
                )

    def finish(unit):
        slot = unit % 2
        mine, start, seen = place(unit)
        context = contract(probs_at[slot, :, :seen], values[:seen, :], 1, 0)
        upstream = tall(up_ref, unit)
        prob_grad = contract(upstream, values[:prefix_len, :], 1, 1)
        for number, head in enumerate(mine):
            out_ref[start : start + ROWS, head * HD : (head + 1) * HD] = context[
                number * ROWS : (number + 1) * ROWS
            ].astype(jnp.bfloat16)
        delta_row = jnp.sum(upstream.astype(jnp.float32) * context, axis=1, keepdims=True)
        score_grad = lead_at[slot] * (prob_grad - delta_row)
        at = pl.ds(unit * tall_rows, tall_rows)
        half_grad[at, :] = score_grad.astype(jnp.bfloat16)
        half_prob[at, :] = probs_at[slot, :, :prefix_len]

    score(0)
    for unit in range(len(units)):
        if unit + 1 < len(units):
            score(unit + 1)
        soften(unit)
        if unit:
            finish(unit - 1)
    finish(len(units) - 1)

    def gathered(ref):
        return jnp.concatenate([tall(ref, unit) for unit in range(len(units))], axis=0)

    key_grad = contract(half_grad[...], gathered(q_ref), 0, 0)
    value_grad = contract(half_prob[...], gathered(up_ref), 0, 0)
    return jnp.concatenate([key_grad * HD**-0.5, value_grad], axis=1)


def fill(keys, values, piece, kv_ref, base, wide):
    size = wide.shape[0]
    prefix_len = keys.shape[0] - size // 2
    keys[:prefix_len, :] = piece[:prefix_len, :HD]
    values[:prefix_len, :] = piece[:prefix_len, HD:]
    pairs = kv_ref[pl.ds(pl.multiple_of(2 * base, size), size), :]
    keys[prefix_len:, :], values[prefix_len:, :] = split_pairs(pairs, wide)


def branch_pass(heads, base, source, pieces, q_ref, kv_ref, up_ref, out_ref, buffers):
    wide, keys, values, *scratch = buffers
    prefix_len = keys.shape[0] - wide.shape[0] // 2
    if len(pieces) == 1:
        fill(keys, values, pieces[0], kv_ref, base, wide)
    else:
        for number, piece in enumerate(pieces):

            @pl.when(source == number)
            def _(piece=piece):
                fill(keys, values, piece, kv_ref, base, wide)

    return head_pass(heads, base, q_ref, up_ref, out_ref, keys, values, scratch, prefix_len)


def own_kernel(heads, answers, branches, later, info, prompts, own_ref, q_ref, kv_ref, up_ref, *refs):
    out_ref, own_grad, *buffers = refs[1:] if later else refs
    base = first_own(prompts, info[0], branches) * answers
    own_grad[...] = branch_pass(
        heads, base, None, [own_ref], q_ref, kv_ref, up_ref, out_ref, buffers
    )


def other_kernel(heads, answers, branches, devices, info, prompts, *refs):
    own_ref, partner_ref, low_ref, high_ref, far_ref = refs[:5]
    q_ref, kv_ref, up_ref, _, out_ref, own_grad, far_grad, grad_ref = refs[5:13]
    *buffers, own_total, far_total = refs[13:]
    step = pl.program_id(0)
    me = info[0]
    branch = other_branch(step, prompts, me, branches)
    source = source_of(prompts[branch], me, devices)
    pieces = [
        own_ref,
        partner_ref,
        low_ref.at[0],
        low_ref.at[1],
        high_ref.at[0],
        high_ref.at[1],
        far_ref,
    ]
    grad = branch_pass(
        heads, branch * answers, source, pieces, q_ref, kv_ref, up_ref, out_ref, buffers
    )
    own_part = jnp.where(source == OWN, grad, 0.0)
    far_part = jnp.where(source == FAR, grad, 0.0)
    grad_ref[step] = grad.astype(jnp.bfloat16)

    @pl.when(step == 0)
    def _():
        own_total[...] = own_part
        far_total[...] = far_part

    @pl.when(step > 0)
    def _():
        own_total[...] += own_part
        far_total[...] += far_part

    @pl.when(step == pl.num_programs(0) - 1)
    def _():
        own_grad[...] = own_total[...]
        far_grad[...] = far_total[...].astype(jnp.bfloat16)


def relay_kernel(branches, devices, info, prompts, grad_ref, got_ref, notes_ref, *outs):
    to_low, to_high, to_me = outs
    me = info[0]
    down, up = lax.rem(me + devices - 2, devices), lax.rem(me + 2, devices)
    low = high = kept = jnp.zeros(grad_ref.shape[1:], jnp.float32)
    notes = notes_ref[...].astype(jnp.float32)
    start = notes.shape[0] - NOTES
    for number in range(branches - 1):
        grad = grad_ref[number].astype(jnp.float32)
        prompt = prompts[other_branch(number, prompts, me, branches)]
        low = low + jnp.where(prompt == down, grad, 0.0)
        high = high + jnp.where(prompt == up, grad, 0.0)
        grad = got_ref[number].astype(jnp.float32)
        prompt = notes[start + number : start + number + 1, :]
        low = low + jnp.where(prompt == down.astype(jnp.float32), grad, 0.0)
        high = high + jnp.where(prompt == up.astype(jnp.float32), grad, 0.0)
        kept = kept + jnp.where(prompt == me.astype(jnp.float32), grad, 0.0)
    to_low[...] = low.astype(jnp.bfloat16)
    to_high[...] = high.astype(jnp.bfloat16)
    to_me[...] = kept


def relay(devices, me, prompts, grad, got, notes):
    branches = prompts.shape[0]
    here = pl.BlockSpec(memory_space=pltpu.VMEM)
    shape = grad.shape[1:]
    return pl.pallas_call(
        functools.partial(relay_kernel, branches, devices),
        grid_spec=pltpu.PrefetchScalarGridSpec(
            num_scalar_prefetch=2, grid=(1,), in_specs=[here] * 3, out_specs=[here] * 3
        ),
        out_shape=[
            jax.ShapeDtypeStruct(shape, jnp.bfloat16),
            jax.ShapeDtypeStruct(shape, jnp.bfloat16),
            jax.ShapeDtypeStruct(shape, jnp.float32),
        ],
        compiler_params=pltpu.CompilerParams(vmem_limit_bytes=VMEM),
        name="relay",
    )(me, prompts, grad, got, notes)


def attention(own, heads, devices, me, prompts, pieces, query, pairs, upstream, out):
    branches = prompts.shape[0]
    answers = query.shape[0] // branches
    prefix_len = pieces[0].shape[0] - NOTES
    width = len(heads) * HD
    steps = 1 if own else branches - 1

    def out_at(step, info, prompts):
        if own:
            return first_own(prompts, info[0], branches), heads[0] // len(heads)
        return other_branch(step, prompts, info[0], branches), 0

    here = pl.BlockSpec(memory_space=pltpu.VMEM)
    there = pl.BlockSpec(memory_space=pl.ANY)
    piece = (prefix_len, 2 * HD)
    operands = [*pieces, query, pairs, upstream]
    in_specs = [here] * len(operands)
    out_shape = [
        jax.ShapeDtypeStruct(query.shape, query.dtype),
        jax.ShapeDtypeStruct(piece, jnp.float32),
    ]
    out_specs = [pl.BlockSpec((answers, width), out_at), here]
    aliases = {}
    if out is not None:
        aliases = {2 + len(operands): 0}
        operands.append(out)
        in_specs.append(there)
    tall_rows = min(TALL, len(heads)) * ROWS
    all_rows = len(heads) * answers
    scratch = [
        pltpu.VMEM((2 * answers, HD), jnp.float32),
        pltpu.VMEM((prefix_len + answers, HD), jnp.bfloat16),
        pltpu.VMEM((prefix_len + answers, HD), jnp.bfloat16),
        pltpu.VMEM((2, tall_rows, prefix_len + answers), jnp.float32),
        pltpu.VMEM((2, tall_rows, prefix_len + answers), jnp.bfloat16),
        pltpu.VMEM((2, tall_rows, prefix_len), jnp.float32),
        pltpu.VMEM((all_rows, prefix_len), jnp.bfloat16),
        pltpu.VMEM((all_rows, prefix_len), jnp.bfloat16),
    ]
    if own:
        body = functools.partial(own_kernel, heads, answers, branches, out is not None)
    else:
        body = functools.partial(other_kernel, heads, answers, branches, devices)
        scratch += [pltpu.VMEM(piece, jnp.float32)] * 2
        for shape in (piece, (steps, *piece)):
            out_shape.append(jax.ShapeDtypeStruct(shape, jnp.bfloat16))
            out_specs.append(here)
    seen = prefix_len + (answers + BLOCK) // 2
    work = steps * answers * width
    return pl.pallas_call(
        body,
        grid_spec=pltpu.PrefetchScalarGridSpec(
            num_scalar_prefetch=2,
            grid=(steps,),
            in_specs=in_specs,
            out_specs=out_specs,
            scratch_shapes=scratch,
        ),
        out_shape=out_shape,
        input_output_aliases=aliases,
        compiler_params=pltpu.CompilerParams(
            dimension_semantics=("arbitrary",), vmem_limit_bytes=VMEM
        ),
        cost_estimate=pl.CostEstimate(
            flops=work * (4 * seen + 6 * prefix_len),
            bytes_accessed=6 * work,
            transcendentals=work // HD * seen,
        ),
        name="own_branch" if own else "other_branches",
    )(me, prompts, *operands)


def shards(prefix, kv_weight, ans_query, ans_kv, d_out, branch_prompt):
    columns = kv_weight.shape[2]
    if columns != HD:
        raise ValueError("one kv head")
    devices = lax.axis_size("dp")
    if devices % 2 or devices < 2 * REACH + 1:
        raise ValueError("dp size")
    if branch_prompt.shape[0] > NOTES or devices > 256:
        raise ValueError("notes size")
    me = lax.axis_index("dp").astype(jnp.int32).reshape(1)
    own_kv = project(me, branch_prompt, prefix[0], kv_weight)
    far = dp_permute(own_kv, far_of)
    partner = dp_permute(own_kv, lambda i: i ^ 1)
    pair = jnp.stack([own_kv, partner])
    low = dp_permute(pair, lambda i: i + 2)
    high = dp_permute(pair, lambda i: i - 2)
    branch = functools.partial(
        attention,
        devices=devices,
        me=me,
        prompts=branch_prompt,
        query=ans_query,
        pairs=ans_kv.reshape(2 * ans_kv.shape[0], HD),
        upstream=d_out,
    )
    heads = tuple(range(ans_query.shape[1] // HD))
    early, late = heads[: len(heads) // 2], heads[len(heads) // 2 :]
    out, early_grad = branch(own=True, heads=early, pieces=[own_kv], out=None)
    out, more_grad, to_far, grad = branch(
        own=False, heads=heads, pieces=[own_kv, partner, low, high, far], out=out
    )
    from_far = dp_permute(to_far, far_of)
    got = dp_permute(grad, lambda i: i ^ 1)
    out, late_grad = branch(own=True, heads=late, pieces=[own_kv], out=out)
    to_low, to_high, to_me = relay(devices, me, branch_prompt, grad, got, partner)
    from_high = dp_permute(to_low, lambda i: i - 2)
    from_low = dp_permute(to_high, lambda i: i + 2)
    grads = [early_grad, late_grad, more_grad, to_me, from_far, from_high, from_low]
    rows = project_back(grads, kv_weight)
    return (out, rows.reshape(1, *rows.shape))


def project_back(grads, kv_weight):
    count = lax.axis_size("tensor")
    if count != 4:
        raise ValueError("tensor size")
    index = lax.axis_index("tensor").astype(jnp.int32).reshape(1)
    far_give, far_keep, near_give, near_keep = back_shares(index, grads, kv_weight, count)

    def swap(x, bit):
        return lax.ppermute(x, "tensor", [(i, i ^ bit) for i in range(count)])

    def both(a, b):
        return a.astype(jnp.float32) + b.astype(jnp.float32)

    far_sum = both(far_keep, swap(far_give, 1)).astype(jnp.bfloat16)
    arrived = swap(far_sum, 2)
    got = swap(near_give, 1)
    mine = lax.optimization_barrier(both(near_keep, got).astype(jnp.bfloat16))
    return both(mine, arrived).astype(jnp.bfloat16)


def solution(mesh):
    return jax.shard_map(
        shards,
        mesh=mesh,
        in_specs=(
            P("dp", None, None),
            P(None, None, "tensor"),
            P("dp", "tensor"),
            P("dp", None, "tensor"),
            P("dp", "tensor"),
            P("dp"),
        ),
        out_specs=(P("dp", "tensor"), P("dp", "tensor", None)),
        check_vma=False,
    )
```

```python
import functools
import math

import jax
import jax.numpy as jnp
from jax import lax
from jax.experimental import pallas as pl
from jax.experimental.pallas import tpu as pltpu
from jax.sharding import PartitionSpec as P

HD = 128
REACH = 3
BLOCK = 128
ROWS = 128
TALL = 4
TILE = 32
CHUNKS = 8
VMEM = 24 << 20
PROJECT_VMEM = 60500000
NOTES = 16
OWN, PARTNER, LOW, LOW_PAIR, HIGH, HIGH_PAIR, FAR = range(7)


def dp_permute(x, target):
    devices = lax.axis_size("dp")
    return lax.ppermute(x, "dp", [(i, target(i) % devices) for i in range(devices)])


def far_of(i):
    return i + REACH if i % 2 else i - REACH


def first_own(prompts, me, branches):
    own = jnp.int32(branches - 1)
    for slot in reversed(range(branches)):
        own = jnp.where(prompts[slot] == me, slot, own)
    return own


def other_branch(step, prompts, me, branches):
    own = first_own(prompts, me, branches)
    return step + jnp.where(step >= own, 1, 0)


def source_of(prompt, me, devices):
    rel = lax.rem(prompt - me + devices, devices)
    rel = jnp.where(rel > REACH, rel - devices, rel)
    odd = lax.rem(me, 2) == 1
    source = jnp.where(rel == 0, OWN, FAR)
    source = jnp.where(rel == -2, LOW, source)
    source = jnp.where(rel == 2, HIGH, source)
    source = jnp.where(rel == 1, jnp.where(odd, HIGH_PAIR, PARTNER), source)
    source = jnp.where(rel == -1, jnp.where(odd, PARTNER, LOW_PAIR), source)
    source = jnp.where(rel == 3, jnp.where(odd, FAR, HIGH_PAIR), source)
    source = jnp.where(rel == -3, jnp.where(odd, LOW_PAIR, FAR), source)
    return source


def contract(a, b, dim_a, dim_b):
    return lax.dot_general(
        a, b, (((dim_a,), (dim_b,)), ((), ())), preferred_element_type=jnp.float32
    )


def split_pairs(pairs, wide):
    rows = pairs.shape[0] // 2
    wide[...] = pairs.astype(jnp.float32)
    return [wide[pl.ds(at, rows, stride=2), :].astype(jnp.bfloat16) for at in range(2)]


def load_split(chunk, pairs, wide, split):
    size = wide.shape[1]
    keys, values = split_pairs(pairs[chunk * size : (chunk + 1) * size, :], wide.at[chunk % 2])
    split[chunk % 2, :, :HD] = keys
    split[chunk % 2, :, HD:] = values


def project_kernel(
    info, prompts, prefix_ref, weight_ref, out_ref, rows, pairs, wide, split, sems
):
    depth = rows.shape[1] // CHUNKS
    copies = []
    for chunk in range(CHUNKS):
        deep = pl.ds(chunk * depth, depth)
        both = pl.ds(chunk * 2 * depth, 2 * depth)
        copies.append(
            (
                pltpu.make_async_copy(weight_ref.at[both, :], pairs.at[both, :], sems.at[0, chunk]),
                pltpu.make_async_copy(prefix_ref.at[:, deep], rows.at[:, deep], sems.at[1, chunk]),
            )
        )
    for pair in copies:
        for copy in pair:
            copy.start()
    total = jnp.zeros((rows.shape[0], out_ref.shape[1]), jnp.float32)
    for chunk in range(CHUNKS + 1):
        if chunk < CHUNKS:
            for copy in copies[chunk]:
                copy.wait()
            load_split(chunk, pairs, wide, split)
        if chunk:
            part = rows[:, (chunk - 1) * depth : chunk * depth]
            total += contract(part, split[(chunk - 1) % 2], 1, 0)
    out_ref[: rows.shape[0], :] = total.astype(out_ref.dtype)
    at = lax.broadcasted_iota(jnp.int32, (NOTES, out_ref.shape[1]), 0)
    notes = jnp.zeros(at.shape, jnp.float32)
    branches = prompts.shape[0]
    own = first_own(prompts, info[0], branches)
    for number in range(branches - 1):
        prompt = jnp.where(number >= own, prompts[number + 1], prompts[number])
        notes = jnp.where(at == number, prompt.astype(jnp.float32), notes)
    out_ref[rows.shape[0] :, :] = notes.astype(out_ref.dtype)


def project(me, prompts, prefix, kv_weight):
    prefix_len, model_width = prefix.shape
    there = pl.BlockSpec(memory_space=pl.ANY)
    return pl.pallas_call(
        project_kernel,
        in_specs=[pl.BlockSpec(memory_space=pltpu.SMEM)] * 2 + [there] * 2,
        out_specs=pl.BlockSpec(memory_space=pltpu.VMEM),
        out_shape=jax.ShapeDtypeStruct((prefix_len + NOTES, 2 * HD), jnp.bfloat16),
        scratch_shapes=[
            pltpu.VMEM(prefix.shape, jnp.bfloat16),
            pltpu.VMEM((2 * model_width, HD), jnp.bfloat16),
            pltpu.VMEM((2, 2 * model_width // CHUNKS, HD), jnp.float32),
            pltpu.VMEM((2, model_width // CHUNKS, 2 * HD), jnp.bfloat16),
            pltpu.SemaphoreType.DMA((2, CHUNKS)),
        ],
        compiler_params=pltpu.CompilerParams(vmem_limit_bytes=PROJECT_VMEM),
        cost_estimate=pl.CostEstimate(
            flops=4 * prefix_len * model_width * HD,
            bytes_accessed=2 * model_width * (prefix_len + 2 * HD),
            transcendentals=0,
        ),
        name="project",
    )(me, prompts, prefix, kv_weight.reshape(2 * model_width, HD))


def back_kernel(index, *refs):
    *grads, weight_ref, far_give, far_keep, near_give, near_keep, wide, split = refs
    depth = far_give.shape[1] // CHUNKS
    rows = far_give.shape[0]
    half, side = index[0] >> 1, index[0] & 1
    owners = (
        2 * (1 - half) + 1 - side,
        2 * (1 - half) + side,
        2 * half + 1 - side,
        2 * half + side,
    )
    parts = []
    for owner in owners:
        at = pl.ds(pl.multiple_of(owner * rows, rows), rows)
        total = grads[0][at, :].astype(jnp.float32)
        for grad in grads[1:]:
            total = total + grad[at, :].astype(jnp.float32)
        parts.append(total.astype(jnp.bfloat16))
    kv_grad = jnp.concatenate(parts, axis=0)
    for chunk in range(CHUNKS + 1):
        if chunk < CHUNKS:
            load_split(chunk, weight_ref, wide, split)
        if chunk:
            share = contract(kv_grad, split[(chunk - 1) % 2], 1, 1).astype(jnp.bfloat16)
            cols = pl.ds((chunk - 1) * depth, depth)
            for number, out in enumerate((far_give, far_keep, near_give, near_keep)):
                out[:, cols] = share[number * rows : (number + 1) * rows]


def back_shares(index, grads, kv_weight, count):
    model_width = kv_weight.shape[0]
    rows = grads[0].shape[0] // count
    here = pl.BlockSpec(memory_space=pltpu.VMEM)
    return pl.pallas_call(
        back_kernel,
        in_specs=[pl.BlockSpec(memory_space=pltpu.SMEM)]
        + [here] * (len(grads) + 1),
        out_specs=[here] * 4,
        out_shape=[jax.ShapeDtypeStruct((rows, model_width), jnp.bfloat16)] * 4,
        scratch_shapes=[
            pltpu.VMEM((2, 2 * model_width // CHUNKS, HD), jnp.float32),
            pltpu.VMEM((2, model_width // CHUNKS, 2 * HD), jnp.bfloat16),
        ],
        compiler_params=pltpu.CompilerParams(vmem_limit_bytes=VMEM),
        cost_estimate=pl.CostEstimate(
            flops=4 * grads[0].shape[0] * model_width * HD,
            bytes_accessed=2 * model_width * (grads[0].shape[0] + 2 * HD),
            transcendentals=0,
        ),
        name="back_shares",
    )(index, *grads, kv_weight.reshape(2 * model_width, HD))


def head_pass(heads, base, q_ref, up_ref, out_ref, keys, values, scratch, prefix_len):
    answers = keys.shape[0] - prefix_len
    scale = HD**-0.5 * math.log2(math.e)
    units = [(at, block) for at in range(0, len(heads), TALL) for block in range(answers // ROWS)]
    scores_at, probs_at, lead_at, half_grad, half_prob = scratch
    tall_rows = min(TALL, len(heads)) * ROWS

    def place(unit):
        at, block = units[unit]
        mine = range(at, min(at + TALL, len(heads)))
        return mine, block * ROWS, prefix_len + (block + 1) * ROWS

    def tall(ref, unit):
        mine, start, _ = place(unit)
        rows = pl.ds(pl.multiple_of(base + start, ROWS), ROWS)
        return jnp.concatenate(
            [ref[rows, heads[at] * HD : (heads[at] + 1) * HD] for at in mine], axis=0
        )

    def score(unit):
        seen = place(unit)[2]
        scores_at[unit % 2, :, :seen] = contract(tall(q_ref, unit), keys[:seen, :], 1, 1)

    def soften(unit):
        slot = unit % 2
        seen = place(unit)[2]
        for tile in range(tall_rows // TILE):
            rows = pl.ds(tile * TILE, TILE)
            first = tile * TILE % ROWS
            edge = seen - ROWS + first // BLOCK * BLOCK
            scores = scores_at[slot, rows, : edge + BLOCK]
            rows_at = lax.broadcasted_iota(jnp.int32, (TILE, BLOCK), 0) + first % BLOCK
            keys_at = lax.broadcasted_iota(jnp.int32, (TILE, BLOCK), 1)
            last = jnp.where(keys_at <= rows_at, scores[:, edge:], -jnp.inf)
            scores = jnp.concatenate([scores[:, :edge], last], axis=1)
            row_max = jnp.max(scores, axis=1, keepdims=True)
            exps = jnp.exp2((scores - row_max) * scale)
            probs = exps * (1.0 / jnp.sum(exps, axis=1, keepdims=True))
            lead_at[slot, rows, :] = probs[:, :prefix_len]
            probs_at[slot, rows, : edge + BLOCK] = probs.astype(jnp.bfloat16)
            if edge + BLOCK < seen:
                probs_at[slot, rows, edge + BLOCK : seen] = jnp.zeros(
                    (TILE, seen - edge - BLOCK), jnp.bfloat16
                )

    def finish(unit):
        slot = unit % 2
        mine, start, seen = place(unit)
        context = contract(probs_at[slot, :, :seen], values[:seen, :], 1, 0)
        upstream = tall(up_ref, unit)
        prob_grad = contract(upstream, values[:prefix_len, :], 1, 1)
        for number, head in enumerate(mine):
            out_ref[start : start + ROWS, head * HD : (head + 1) * HD] = context[
                number * ROWS : (number + 1) * ROWS
            ].astype(jnp.bfloat16)
        delta_row = jnp.sum(upstream.astype(jnp.float32) * context, axis=1, keepdims=True)
        score_grad = lead_at[slot] * (prob_grad - delta_row)
        at = pl.ds(unit * tall_rows, tall_rows)
        half_grad[at, :] = score_grad.astype(jnp.bfloat16)
        half_prob[at, :] = probs_at[slot, :, :prefix_len]

    score(0)
    for unit in range(len(units)):
        if unit + 1 < len(units):
            score(unit + 1)
        soften(unit)
        if unit:
            finish(unit - 1)
    finish(len(units) - 1)

    def gathered(ref):
        return jnp.concatenate([tall(ref, unit) for unit in range(len(units))], axis=0)

    key_grad = contract(half_grad[...], gathered(q_ref), 0, 0)
    value_grad = contract(half_prob[...], gathered(up_ref), 0, 0)
    return jnp.concatenate([key_grad * HD**-0.5, value_grad], axis=1)


def fill(keys, values, piece, kv_ref, base, wide):
    size = wide.shape[0]
    prefix_len = keys.shape[0] - size // 2
    keys[:prefix_len, :] = piece[:prefix_len, :HD]
    values[:prefix_len, :] = piece[:prefix_len, HD:]
    pairs = kv_ref[pl.ds(pl.multiple_of(2 * base, size), size), :]
    keys[prefix_len:, :], values[prefix_len:, :] = split_pairs(pairs, wide)


def branch_pass(heads, base, source, pieces, q_ref, kv_ref, up_ref, out_ref, buffers):
    wide, keys, values, *scratch = buffers
    prefix_len = keys.shape[0] - wide.shape[0] // 2
    if len(pieces) == 1:
        fill(keys, values, pieces[0], kv_ref, base, wide)
    else:
        for number, piece in enumerate(pieces):

            @pl.when(source == number)
            def _(piece=piece):
                fill(keys, values, piece, kv_ref, base, wide)

    return head_pass(heads, base, q_ref, up_ref, out_ref, keys, values, scratch, prefix_len)


def own_kernel(heads, answers, branches, later, info, prompts, own_ref, q_ref, kv_ref, up_ref, *refs):
    out_ref, own_grad, *buffers = refs[1:] if later else refs
    base = first_own(prompts, info[0], branches) * answers
    own_grad[...] = branch_pass(
        heads, base, None, [own_ref], q_ref, kv_ref, up_ref, out_ref, buffers
    )


def other_kernel(heads, answers, branches, devices, info, prompts, *refs):
    own_ref, partner_ref, low_ref, high_ref, far_ref = refs[:5]
    q_ref, kv_ref, up_ref, _, out_ref, own_grad, far_grad, grad_ref = refs[5:13]
    *buffers, own_total, far_total = refs[13:]
    step = pl.program_id(0)
    me = info[0]
    branch = other_branch(step, prompts, me, branches)
    source = source_of(prompts[branch], me, devices)
    pieces = [
        own_ref,
        partner_ref,
        low_ref.at[0],
        low_ref.at[1],
        high_ref.at[0],
        high_ref.at[1],
        far_ref,
    ]
    grad = branch_pass(
        heads, branch * answers, source, pieces, q_ref, kv_ref, up_ref, out_ref, buffers
    )
    own_part = jnp.where(source == OWN, grad, 0.0)
    far_part = jnp.where(source == FAR, grad, 0.0)
    grad_ref[step] = grad.astype(jnp.bfloat16)

    @pl.when(step == 0)
    def _():
        own_total[...] = own_part
        far_total[...] = far_part

    @pl.when(step > 0)
    def _():
        own_total[...] += own_part
        far_total[...] += far_part

    @pl.when(step == pl.num_programs(0) - 1)
    def _():
        own_grad[...] = own_total[...]
        far_grad[...] = far_total[...].astype(jnp.bfloat16)


def relay_kernel(branches, devices, info, prompts, grad_ref, got_ref, notes_ref, *outs):
    to_low, to_high, to_me = outs
    me = info[0]
    down, up = lax.rem(me + devices - 2, devices), lax.rem(me + 2, devices)
    low = high = kept = jnp.zeros(grad_ref.shape[1:], jnp.float32)
    notes = notes_ref[...].astype(jnp.float32)
    start = notes.shape[0] - NOTES
    for number in range(branches - 1):
        grad = grad_ref[number].astype(jnp.float32)
        prompt = prompts[other_branch(number, prompts, me, branches)]
        low = low + jnp.where(prompt == down, grad, 0.0)
        high = high + jnp.where(prompt == up, grad, 0.0)
        grad = got_ref[number].astype(jnp.float32)
        prompt = notes[start + number : start + number + 1, :]
        low = low + jnp.where(prompt == down.astype(jnp.float32), grad, 0.0)
        high = high + jnp.where(prompt == up.astype(jnp.float32), grad, 0.0)
        kept = kept + jnp.where(prompt == me.astype(jnp.float32), grad, 0.0)
    to_low[...] = low.astype(jnp.bfloat16)
    to_high[...] = high.astype(jnp.bfloat16)
    to_me[...] = kept


def relay(devices, me, prompts, grad, got, notes):
    branches = prompts.shape[0]
    here = pl.BlockSpec(memory_space=pltpu.VMEM)
    shape = grad.shape[1:]
    return pl.pallas_call(
        functools.partial(relay_kernel, branches, devices),
        grid_spec=pltpu.PrefetchScalarGridSpec(
            num_scalar_prefetch=2, grid=(1,), in_specs=[here] * 3, out_specs=[here] * 3
        ),
        out_shape=[
            jax.ShapeDtypeStruct(shape, jnp.bfloat16),
            jax.ShapeDtypeStruct(shape, jnp.bfloat16),
            jax.ShapeDtypeStruct(shape, jnp.float32),
        ],
        compiler_params=pltpu.CompilerParams(vmem_limit_bytes=VMEM),
        name="relay",
    )(me, prompts, grad, got, notes)


def attention(own, heads, devices, me, prompts, pieces, query, pairs, upstream, out):
    branches = prompts.shape[0]
    answers = query.shape[0] // branches
    prefix_len = pieces[0].shape[0] - NOTES
    width = len(heads) * HD
    steps = 1 if own else branches - 1

    def out_at(step, info, prompts):
        if own:
            return first_own(prompts, info[0], branches), heads[0] // len(heads)
        return other_branch(step, prompts, info[0], branches), 0

    here = pl.BlockSpec(memory_space=pltpu.VMEM)
    there = pl.BlockSpec(memory_space=pl.ANY)
    piece = (prefix_len, 2 * HD)
    operands = [*pieces, query, pairs, upstream]
    in_specs = [here] * len(operands)
    out_shape = [
        jax.ShapeDtypeStruct(query.shape, query.dtype),
        jax.ShapeDtypeStruct(piece, jnp.float32),
    ]
    out_specs = [pl.BlockSpec((answers, width), out_at), here]
    aliases = {}
    if out is not None:
        aliases = {2 + len(operands): 0}
        operands.append(out)
        in_specs.append(there)
    tall_rows = min(TALL, len(heads)) * ROWS
    all_rows = len(heads) * answers
    scratch = [
        pltpu.VMEM((2 * answers, HD), jnp.float32),
        pltpu.VMEM((prefix_len + answers, HD), jnp.bfloat16),
        pltpu.VMEM((prefix_len + answers, HD), jnp.bfloat16),
        pltpu.VMEM((2, tall_rows, prefix_len + answers), jnp.float32),
        pltpu.VMEM((2, tall_rows, prefix_len + answers), jnp.bfloat16),
        pltpu.VMEM((2, tall_rows, prefix_len), jnp.float32),
        pltpu.VMEM((all_rows, prefix_len), jnp.bfloat16),
        pltpu.VMEM((all_rows, prefix_len), jnp.bfloat16),
    ]
    if own:
        body = functools.partial(own_kernel, heads, answers, branches, out is not None)
    else:
        body = functools.partial(other_kernel, heads, answers, branches, devices)
        scratch += [pltpu.VMEM(piece, jnp.float32)] * 2
        for shape in (piece, (steps, *piece)):
            out_shape.append(jax.ShapeDtypeStruct(shape, jnp.bfloat16))
            out_specs.append(here)
    seen = prefix_len + (answers + BLOCK) // 2
    work = steps * answers * width
    return pl.pallas_call(
        body,
        grid_spec=pltpu.PrefetchScalarGridSpec(
            num_scalar_prefetch=2,
            grid=(steps,),
            in_specs=in_specs,
            out_specs=out_specs,
            scratch_shapes=scratch,
        ),
        out_shape=out_shape,
        input_output_aliases=aliases,
        compiler_params=pltpu.CompilerParams(
            dimension_semantics=("arbitrary",), vmem_limit_bytes=VMEM
        ),
        cost_estimate=pl.CostEstimate(
            flops=work * (4 * seen + 6 * prefix_len),
            bytes_accessed=6 * work,
            transcendentals=work // HD * seen,
        ),
        name="own_branch" if own else "other_branches",
    )(me, prompts, *operands)


def shards(prefix, kv_weight, ans_query, ans_kv, d_out, branch_prompt):
    columns = kv_weight.shape[2]
    if columns != HD:
        raise ValueError("one kv head")
    devices = lax.axis_size("dp")
    if devices % 2 or devices < 2 * REACH + 1:
        raise ValueError("dp size")
    if branch_prompt.shape[0] > NOTES or devices > 256:
        raise ValueError("notes size")
    me = lax.axis_index("dp").astype(jnp.int32).reshape(1)
    answer_pairs = ans_kv.reshape(2 * ans_kv.shape[0], HD)
    own_kv = project(me, branch_prompt, prefix[0], kv_weight)
    partner = dp_permute(own_kv, lambda i: i ^ 1)
    far = dp_permute(own_kv, far_of)
    pair = jnp.stack([own_kv, partner])
    low = dp_permute(pair, lambda i: i + 2)
    high = dp_permute(pair, lambda i: i - 2)
    branch = functools.partial(
        attention,
        devices=devices,
        me=me,
        prompts=branch_prompt,
        query=ans_query,
        pairs=answer_pairs,
        upstream=d_out,
    )
    heads = tuple(range(ans_query.shape[1] // HD))
    early, late = heads[: len(heads) // 2], heads[len(heads) // 2 :]
    out, early_grad = branch(own=True, heads=early, pieces=[own_kv], out=None)
    out, more_grad, to_far, grad = branch(
        own=False, heads=heads, pieces=[own_kv, partner, low, high, far], out=out
    )
    from_far = dp_permute(to_far, far_of)
    got = dp_permute(grad, lambda i: i ^ 1)
    out, late_grad = branch(own=True, heads=late, pieces=[own_kv], out=out)
    to_low, to_high, to_me = relay(devices, me, branch_prompt, grad, got, partner)
    from_high = dp_permute(to_low, lambda i: i - 2)
    from_low = dp_permute(to_high, lambda i: i + 2)
    grads = [early_grad, late_grad, more_grad, to_me, from_far, from_high, from_low]
    rows = project_back(grads, kv_weight)
    return (out, rows.reshape(1, *rows.shape))


def project_back(grads, kv_weight):
    count = lax.axis_size("tensor")
    if count != 4:
        raise ValueError("tensor size")
    index = lax.axis_index("tensor").astype(jnp.int32).reshape(1)
    far_give, far_keep, near_give, near_keep = back_shares(index, grads, kv_weight, count)

    def swap(x, bit):
        return lax.ppermute(x, "tensor", [(i, i ^ bit) for i in range(count)])

    def both(a, b):
        return a.astype(jnp.float32) + b.astype(jnp.float32)

    far_sum = both(far_keep, swap(far_give, 1)).astype(jnp.bfloat16)
    arrived = swap(far_sum, 2)
    got = swap(near_give, 1)
    mine = lax.optimization_barrier(both(near_keep, got).astype(jnp.bfloat16))
    return both(mine, arrived).astype(jnp.bfloat16)


def solution(mesh):
    return jax.shard_map(
        shards,
        mesh=mesh,
        in_specs=(
            P("dp", None, None),
            P(None, None, "tensor"),
            P("dp", "tensor"),
            P("dp", None, "tensor"),
            P("dp", "tensor"),
            P("dp"),
        ),
        out_specs=(P("dp", "tensor"), P("dp", "tensor", None)),
        check_vma=False,
    )
```

```python
import functools
import math

import jax
import jax.numpy as jnp
from jax import lax
from jax.experimental import pallas as pl
from jax.experimental.pallas import tpu as pltpu
from jax.sharding import PartitionSpec as P

HD = 128
REACH = 3
BLOCK = 128
ROWS = 128
TALL = 4
TILE = 32
CHUNKS = 8
VMEM = 24 << 20
PARTS = 2
PROJECT_VMEM = 54500000
NOTES = 16
OWN, PARTNER, LOW, LOW_PAIR, HIGH, HIGH_PAIR, FAR = range(7)


def dp_permute(x, target):
    devices = lax.axis_size("dp")
    return lax.ppermute(x, "dp", [(i, target(i) % devices) for i in range(devices)])


def far_of(i):
    return i + REACH if i % 2 else i - REACH


def first_own(prompts, me, branches):
    own = jnp.int32(branches - 1)
    for slot in reversed(range(branches)):
        own = jnp.where(prompts[slot] == me, slot, own)
    return own


def other_branch(step, prompts, me, branches):
    own = first_own(prompts, me, branches)
    return step + jnp.where(step >= own, 1, 0)


def source_of(prompt, me, devices):
    rel = lax.rem(prompt - me + devices, devices)
    rel = jnp.where(rel > REACH, rel - devices, rel)
    odd = lax.rem(me, 2) == 1
    source = jnp.where(rel == 0, OWN, FAR)
    source = jnp.where(rel == -2, LOW, source)
    source = jnp.where(rel == 2, HIGH, source)
    source = jnp.where(rel == 1, jnp.where(odd, HIGH_PAIR, PARTNER), source)
    source = jnp.where(rel == -1, jnp.where(odd, PARTNER, LOW_PAIR), source)
    source = jnp.where(rel == 3, jnp.where(odd, FAR, HIGH_PAIR), source)
    source = jnp.where(rel == -3, jnp.where(odd, LOW_PAIR, FAR), source)
    return source


def contract(a, b, dim_a, dim_b):
    return lax.dot_general(
        a, b, (((dim_a,), (dim_b,)), ((), ())), preferred_element_type=jnp.float32
    )


def split_pairs(pairs, wide):
    rows = pairs.shape[0] // 2
    wide[...] = pairs.astype(jnp.float32)
    return [wide[pl.ds(at, rows, stride=2), :].astype(jnp.bfloat16) for at in range(2)]


def load_split(chunk, pairs, wide, split):
    size = wide.shape[1]
    keys, values = split_pairs(pairs[chunk * size : (chunk + 1) * size, :], wide.at[chunk % 2])
    split[chunk % 2, :, :HD] = keys
    split[chunk % 2, :, HD:] = values


def project_kernel(prefix_ref, weight_ref, out_ref, rows, pairs, wide, split, sems):
    depth = rows.shape[1] // CHUNKS
    copies = []
    for chunk in range(CHUNKS):
        deep = pl.ds(chunk * depth, depth)
        both = pl.ds(chunk * 2 * depth, 2 * depth)
        copies.append(
            (
                pltpu.make_async_copy(weight_ref.at[both, :], pairs.at[both, :], sems.at[0, chunk]),
                pltpu.make_async_copy(prefix_ref.at[:, deep], rows.at[:, deep], sems.at[1, chunk]),
            )
        )
    for pair in copies:
        for copy in pair:
            copy.start()
    total = jnp.zeros((rows.shape[0], out_ref.shape[1]), jnp.float32)
    for chunk in range(CHUNKS + 1):
        if chunk < CHUNKS:
            for copy in copies[chunk]:
                copy.wait()
            load_split(chunk, pairs, wide, split)
        if chunk:
            part = rows[:, (chunk - 1) * depth : chunk * depth]
            total += contract(part, split[(chunk - 1) % 2], 1, 0)
    out_ref[...] = total.astype(out_ref.dtype)


def project(prefix, kv_weight):
    prefix_len, model_width = prefix.shape
    there = pl.BlockSpec(memory_space=pl.ANY)
    return pl.pallas_call(
        project_kernel,
        in_specs=[there] * 2,
        out_specs=pl.BlockSpec(memory_space=pltpu.VMEM),
        out_shape=jax.ShapeDtypeStruct((prefix_len, 2 * HD), jnp.bfloat16),
        scratch_shapes=[
            pltpu.VMEM(prefix.shape, jnp.bfloat16),
            pltpu.VMEM((2 * model_width, HD), jnp.bfloat16),
            pltpu.VMEM((2, 2 * model_width // CHUNKS, HD), jnp.float32),
            pltpu.VMEM((2, model_width // CHUNKS, 2 * HD), jnp.bfloat16),
            pltpu.SemaphoreType.DMA((2, CHUNKS)),
        ],
        compiler_params=pltpu.CompilerParams(vmem_limit_bytes=PROJECT_VMEM),
        cost_estimate=pl.CostEstimate(
            flops=4 * prefix_len * model_width * HD,
            bytes_accessed=2 * model_width * (prefix_len + 2 * HD),
            transcendentals=0,
        ),
        name="project",
    )(prefix, kv_weight.reshape(2 * model_width, HD))


def back_kernel(part, index, *refs):
    *grads, weight_ref, far_give, far_keep, near_give, near_keep, wide, split = refs
    depth = split.shape[1]
    chunks = far_give.shape[1] // depth
    rows = far_give.shape[0]
    half, side = index[0] >> 1, index[0] & 1
    owners = (
        2 * (1 - half) + 1 - side,
        2 * (1 - half) + side,
        2 * half + 1 - side,
        2 * half + side,
    )
    parts = []
    for owner in owners:
        at = pl.ds(pl.multiple_of(owner * rows, rows), rows)
        total = grads[0][at, :].astype(jnp.float32)
        for grad in grads[1:]:
            total = total + grad[at, :].astype(jnp.float32)
        parts.append(total.astype(jnp.bfloat16))
    kv_grad = jnp.concatenate(parts, axis=0)
    for chunk in range(chunks + 1):
        if chunk < chunks:
            load_split(part * chunks + chunk, weight_ref, wide, split)
        if chunk:
            share = contract(kv_grad, split[(part * chunks + chunk - 1) % 2], 1, 1).astype(jnp.bfloat16)
            cols = pl.ds((chunk - 1) * depth, depth)
            for number, out in enumerate((far_give, far_keep, near_give, near_keep)):
                out[:, cols] = share[number * rows : (number + 1) * rows]


def back_shares(index, grads, kv_weight, count, part):
    model_width = kv_weight.shape[0]
    rows = grads[0].shape[0] // count
    here = pl.BlockSpec(memory_space=pltpu.VMEM)
    return pl.pallas_call(
        functools.partial(back_kernel, part),
        in_specs=[pl.BlockSpec(memory_space=pltpu.SMEM)]
        + [here] * (len(grads) + 1),
        out_specs=[here] * 4,
        out_shape=[jax.ShapeDtypeStruct((rows, model_width // PARTS), jnp.bfloat16)] * 4,
        scratch_shapes=[
            pltpu.VMEM((2, 2 * model_width // CHUNKS, HD), jnp.float32),
            pltpu.VMEM((2, model_width // CHUNKS, 2 * HD), jnp.bfloat16),
        ],
        compiler_params=pltpu.CompilerParams(vmem_limit_bytes=VMEM),
        cost_estimate=pl.CostEstimate(
            flops=4 * grads[0].shape[0] * model_width * HD // PARTS,
            bytes_accessed=2 * model_width * (grads[0].shape[0] + 2 * HD) // PARTS,
            transcendentals=0,
        ),
        name="back_shares",
    )(index, *grads, kv_weight.reshape(2 * model_width, HD))


def head_pass(heads, base, q_ref, up_ref, out_ref, keys, values, scratch, prefix_len):
    answers = keys.shape[0] - prefix_len
    scale = HD**-0.5 * math.log2(math.e)
    units = [(at, block) for at in range(0, len(heads), TALL) for block in range(answers // ROWS)]
    scores_at, probs_at, lead_at, half_grad, half_prob = scratch
    tall_rows = min(TALL, len(heads)) * ROWS

    def place(unit):
        at, block = units[unit]
        mine = range(at, min(at + TALL, len(heads)))
        return mine, block * ROWS, prefix_len + (block + 1) * ROWS

    def tall(ref, unit):
        mine, start, _ = place(unit)
        rows = pl.ds(pl.multiple_of(base + start, ROWS), ROWS)
        return jnp.concatenate(
            [ref[rows, heads[at] * HD : (heads[at] + 1) * HD] for at in mine], axis=0
        )

    def score(unit):
        seen = place(unit)[2]
        scores_at[unit % 2, :, :seen] = contract(tall(q_ref, unit), keys[:seen, :], 1, 1)

    def soften(unit):
        slot = unit % 2
        seen = place(unit)[2]
        for tile in range(tall_rows // TILE):
            rows = pl.ds(tile * TILE, TILE)
            first = tile * TILE % ROWS
            edge = seen - ROWS + first // BLOCK * BLOCK
            scores = scores_at[slot, rows, : edge + BLOCK]
            rows_at = lax.broadcasted_iota(jnp.int32, (TILE, BLOCK), 0) + first % BLOCK
            keys_at = lax.broadcasted_iota(jnp.int32, (TILE, BLOCK), 1)
            last = jnp.where(keys_at <= rows_at, scores[:, edge:], -jnp.inf)
            scores = jnp.concatenate([scores[:, :edge], last], axis=1)
            row_max = jnp.max(scores, axis=1, keepdims=True)
            exps = jnp.exp2((scores - row_max) * scale)
            probs = exps * (1.0 / jnp.sum(exps, axis=1, keepdims=True))
            lead_at[slot, rows, :] = probs[:, :prefix_len]
            probs_at[slot, rows, : edge + BLOCK] = probs.astype(jnp.bfloat16)
            if edge + BLOCK < seen:
                probs_at[slot, rows, edge + BLOCK : seen] = jnp.zeros(
                    (TILE, seen - edge - BLOCK), jnp.bfloat16
                )

    def finish(unit):
        slot = unit % 2
        mine, start, seen = place(unit)
        context = contract(probs_at[slot, :, :seen], values[:seen, :], 1, 0)
        upstream = tall(up_ref, unit)
        prob_grad = contract(upstream, values[:prefix_len, :], 1, 1)
        for number, head in enumerate(mine):
            out_ref[start : start + ROWS, head * HD : (head + 1) * HD] = context[
                number * ROWS : (number + 1) * ROWS
            ].astype(jnp.bfloat16)
        delta_row = jnp.sum(upstream.astype(jnp.float32) * context, axis=1, keepdims=True)
        score_grad = lead_at[slot] * (prob_grad - delta_row)
        at = pl.ds(unit * tall_rows, tall_rows)
        half_grad[at, :] = score_grad.astype(jnp.bfloat16)
        half_prob[at, :] = probs_at[slot, :, :prefix_len]

    score(0)
    for unit in range(len(units)):
        if unit + 1 < len(units):
            score(unit + 1)
        soften(unit)
        if unit:
            finish(unit - 1)
    finish(len(units) - 1)

    def gathered(ref):
        return jnp.concatenate([tall(ref, unit) for unit in range(len(units))], axis=0)

    key_grad = contract(half_grad[...], gathered(q_ref), 0, 0)
    value_grad = contract(half_prob[...], gathered(up_ref), 0, 0)
    return jnp.concatenate([key_grad * HD**-0.5, value_grad], axis=1)


def fill(keys, values, piece, kv_ref, base, wide):
    size = wide.shape[0]
    prefix_len = keys.shape[0] - size // 2
    keys[:prefix_len, :] = piece[:, :HD]
    values[:prefix_len, :] = piece[:, HD:]
    pairs = kv_ref[pl.ds(pl.multiple_of(2 * base, size), size), :]
    keys[prefix_len:, :], values[prefix_len:, :] = split_pairs(pairs, wide)


def branch_pass(heads, base, source, pieces, q_ref, kv_ref, up_ref, out_ref, buffers):
    wide, keys, values, *scratch = buffers
    prefix_len = keys.shape[0] - wide.shape[0] // 2
    if len(pieces) == 1:
        fill(keys, values, pieces[0], kv_ref, base, wide)
    else:
        for number, piece in enumerate(pieces):

            @pl.when(source == number)
            def _(piece=piece):
                fill(keys, values, piece, kv_ref, base, wide)

    return head_pass(heads, base, q_ref, up_ref, out_ref, keys, values, scratch, prefix_len)


def own_kernel(heads, answers, branches, later, info, prompts, own_ref, q_ref, kv_ref, up_ref, *refs):
    out_ref, own_grad, *buffers = refs[1:] if later else refs
    base = first_own(prompts, info[0], branches) * answers
    own_grad[...] = branch_pass(
        heads, base, None, [own_ref], q_ref, kv_ref, up_ref, out_ref, buffers
    )


def other_kernel(heads, answers, branches, devices, info, prompts, *refs):
    own_ref, partner_ref, low_ref, high_ref, far_ref = refs[:5]
    q_ref, kv_ref, up_ref, _, out_ref, own_grad, far_grad, grad_ref = refs[5:13]
    *buffers, own_total, far_total = refs[13:]
    step = pl.program_id(0)
    me = info[0]
    branch = other_branch(step, prompts, me, branches)
    source = source_of(prompts[branch], me, devices)
    pieces = [
        own_ref,
        partner_ref,
        low_ref.at[0],
        low_ref.at[1],
        high_ref.at[0],
        high_ref.at[1],
        far_ref,
    ]
    grad = branch_pass(
        heads, branch * answers, source, pieces, q_ref, kv_ref, up_ref, out_ref, buffers
    )
    own_part = jnp.where(source == OWN, grad, 0.0)
    far_part = jnp.where(source == FAR, grad, 0.0)
    prefix_len = grad.shape[0]
    grad_ref[step, :prefix_len, :] = grad.astype(jnp.bfloat16)
    prompt = prompts[branch].astype(jnp.float32)
    grad_ref[step, prefix_len:, :] = jnp.full((NOTES, grad.shape[1]), prompt).astype(jnp.bfloat16)

    @pl.when(step == 0)
    def _():
        own_total[...] = own_part
        far_total[...] = far_part

    @pl.when(step > 0)
    def _():
        own_total[...] += own_part
        far_total[...] += far_part

    @pl.when(step == pl.num_programs(0) - 1)
    def _():
        own_grad[...] = own_total[...]
        far_grad[...] = far_total[...].astype(jnp.bfloat16)


def relay_kernel(branches, devices, info, prompts, grad_ref, got_ref, *outs):
    to_low, to_high, to_me = outs
    me = info[0]
    down, up = lax.rem(me + devices - 2, devices), lax.rem(me + 2, devices)
    low = high = kept = jnp.zeros(to_me.shape, jnp.float32)
    prefix_len = to_me.shape[0]
    for number in range(branches - 1):
        grad = grad_ref[number, :prefix_len, :].astype(jnp.float32)
        prompt = prompts[other_branch(number, prompts, me, branches)]
        low = low + jnp.where(prompt == down, grad, 0.0)
        high = high + jnp.where(prompt == up, grad, 0.0)
        grad = got_ref[number, :prefix_len, :].astype(jnp.float32)
        prompt = got_ref[number, prefix_len : prefix_len + NOTES, :].astype(jnp.float32)[:1]
        low = low + jnp.where(prompt == down.astype(jnp.float32), grad, 0.0)
        high = high + jnp.where(prompt == up.astype(jnp.float32), grad, 0.0)
        kept = kept + jnp.where(prompt == me.astype(jnp.float32), grad, 0.0)
    to_low[...] = low.astype(jnp.bfloat16)
    to_high[...] = high.astype(jnp.bfloat16)
    to_me[...] = kept


def relay(devices, me, prompts, grad, got):
    branches = prompts.shape[0]
    here = pl.BlockSpec(memory_space=pltpu.VMEM)
    shape = (grad.shape[1] - NOTES, grad.shape[2])
    return pl.pallas_call(
        functools.partial(relay_kernel, branches, devices),
        grid_spec=pltpu.PrefetchScalarGridSpec(
            num_scalar_prefetch=2, grid=(1,), in_specs=[here] * 2, out_specs=[here] * 3
        ),
        out_shape=[
            jax.ShapeDtypeStruct(shape, jnp.bfloat16),
            jax.ShapeDtypeStruct(shape, jnp.bfloat16),
            jax.ShapeDtypeStruct(shape, jnp.float32),
        ],
        compiler_params=pltpu.CompilerParams(vmem_limit_bytes=VMEM),
        name="relay",
    )(me, prompts, grad, got)


def attention(own, heads, devices, me, prompts, pieces, query, pairs, upstream, out):
    branches = prompts.shape[0]
    answers = query.shape[0] // branches
    prefix_len = pieces[0].shape[0]
    width = len(heads) * HD
    steps = 1 if own else branches - 1

    def out_at(step, info, prompts):
        if own:
            return first_own(prompts, info[0], branches), heads[0] // len(heads)
        return other_branch(step, prompts, info[0], branches), 0

    here = pl.BlockSpec(memory_space=pltpu.VMEM)
    there = pl.BlockSpec(memory_space=pl.ANY)
    piece = (prefix_len, 2 * HD)
    operands = [*pieces, query, pairs, upstream]
    in_specs = [here] * len(operands)
    out_shape = [
        jax.ShapeDtypeStruct(query.shape, query.dtype),
        jax.ShapeDtypeStruct(piece, jnp.float32),
    ]
    out_specs = [pl.BlockSpec((answers, width), out_at), here]
    aliases = {}
    if out is not None:
        aliases = {2 + len(operands): 0}
        operands.append(out)
        in_specs.append(there)
    tall_rows = min(TALL, len(heads)) * ROWS
    all_rows = len(heads) * answers
    scratch = [
        pltpu.VMEM((2 * answers, HD), jnp.float32),
        pltpu.VMEM((prefix_len + answers, HD), jnp.bfloat16),
        pltpu.VMEM((prefix_len + answers, HD), jnp.bfloat16),
        pltpu.VMEM((2, tall_rows, prefix_len + answers), jnp.float32),
        pltpu.VMEM((2, tall_rows, prefix_len + answers), jnp.bfloat16),
        pltpu.VMEM((2, tall_rows, prefix_len), jnp.float32),
        pltpu.VMEM((all_rows, prefix_len), jnp.bfloat16),
        pltpu.VMEM((all_rows, prefix_len), jnp.bfloat16),
    ]
    if own:
        body = functools.partial(own_kernel, heads, answers, branches, out is not None)
    else:
        body = functools.partial(other_kernel, heads, answers, branches, devices)
        scratch += [pltpu.VMEM(piece, jnp.float32)] * 2
        for shape in (piece, (steps, prefix_len + NOTES, 2 * HD)):
            out_shape.append(jax.ShapeDtypeStruct(shape, jnp.bfloat16))
            out_specs.append(here)
    seen = prefix_len + (answers + BLOCK) // 2
    work = steps * answers * width
    return pl.pallas_call(
        body,
        grid_spec=pltpu.PrefetchScalarGridSpec(
            num_scalar_prefetch=2,
            grid=(steps,),
            in_specs=in_specs,
            out_specs=out_specs,
            scratch_shapes=scratch,
        ),
        out_shape=out_shape,
        input_output_aliases=aliases,
        compiler_params=pltpu.CompilerParams(
            dimension_semantics=("arbitrary",), vmem_limit_bytes=VMEM
        ),
        cost_estimate=pl.CostEstimate(
            flops=work * (4 * seen + 6 * prefix_len),
            bytes_accessed=6 * work,
            transcendentals=work // HD * seen,
        ),
        name="own_branch" if own else "other_branches",
    )(me, prompts, *operands)


def shards(prefix, kv_weight, ans_query, ans_kv, d_out, branch_prompt):
    columns = kv_weight.shape[2]
    if columns != HD:
        raise ValueError("one kv head")
    devices = lax.axis_size("dp")
    if devices % 2 or devices < 2 * REACH + 1:
        raise ValueError("dp size")
    if devices > 256:
        raise ValueError("notes size")
    me = lax.axis_index("dp").astype(jnp.int32).reshape(1)
    answer_pairs = ans_kv.reshape(2 * ans_kv.shape[0], HD)
    own_kv = project(prefix[0], kv_weight)
    partner = dp_permute(own_kv, lambda i: i ^ 1)
    far = dp_permute(own_kv, far_of)
    pair = jnp.stack([own_kv, partner])
    low = dp_permute(pair, lambda i: i + 2)
    high = dp_permute(pair, lambda i: i - 2)
    branch = functools.partial(
        attention,
        devices=devices,
        me=me,
        prompts=branch_prompt,
        query=ans_query,
        pairs=answer_pairs,
        upstream=d_out,
    )
    heads = tuple(range(ans_query.shape[1] // HD))
    early, late = heads[: len(heads) // 2], heads[len(heads) // 2 :]
    out, early_grad = branch(own=True, heads=early, pieces=[own_kv], out=None)
    out, more_grad, to_far, grad = branch(
        own=False, heads=heads, pieces=[own_kv, partner, low, high, far], out=out
    )
    from_far = dp_permute(to_far, far_of)
    got = dp_permute(grad, lambda i: i ^ 1)
    out, late_grad = branch(own=True, heads=late, pieces=[own_kv], out=out)
    to_low, to_high, to_me = relay(devices, me, branch_prompt, grad, got)
    from_high = dp_permute(to_low, lambda i: i - 2)
    from_low = dp_permute(to_high, lambda i: i + 2)
    grads = [early_grad, late_grad, more_grad, to_me, from_far, from_high, from_low]
    rows = project_back(grads, kv_weight)
    return (out, rows.reshape(1, *rows.shape))


def project_back(grads, kv_weight):
    count = lax.axis_size("tensor")
    if count != 4:
        raise ValueError("tensor size")
    index = lax.axis_index("tensor").astype(jnp.int32).reshape(1)

    def swap(x, bit):
        return lax.ppermute(x, "tensor", [(i, i ^ bit) for i in range(count)])

    def both(a, b):
        return (a.astype(jnp.float32) + b.astype(jnp.float32)).astype(jnp.bfloat16)

    shares = [back_shares(index, grads, kv_weight, count, part) for part in range(PARTS)]
    arrived, mine = [], []
    for far_give, far_keep, _, _ in shares:
        got = swap(far_give, 1)
        arrived.append(swap(both(far_keep, got), 2))
    for _, _, near_give, near_keep in shares:
        got = swap(near_give, 1)
        mine.append(lax.optimization_barrier(both(near_keep, got)))
    return jnp.concatenate([both(a, b) for a, b in zip(mine, arrived)], axis=1)


def solution(mesh):
    return jax.shard_map(
        shards,
        mesh=mesh,
        in_specs=(
            P("dp", None, None),
            P(None, None, "tensor"),
            P("dp", "tensor"),
            P("dp", None, "tensor"),
            P("dp", "tensor"),
            P("dp"),
        ),
        out_specs=(P("dp", "tensor"), P("dp", "tensor", None)),
        check_vma=False,
    )
```

```python
import functools
import math

import jax
import jax.numpy as jnp
from jax import lax
from jax.experimental import pallas as pl
from jax.experimental.pallas import tpu as pltpu
from jax.sharding import PartitionSpec as P

HD = 128
REACH = 3
BLOCK = 128
ROWS = 128
TALL = 4
TILE = 32
CHUNKS = 8
VMEM = 24 << 20
PARTS = 2
PROJECT_VMEM = 54500000
NOTES = 16
OWN, PARTNER, LOW, LOW_PAIR, HIGH, HIGH_PAIR, FAR, SOURCES = range(8)


def dp_permute(x, target):
    devices = lax.axis_size("dp")
    return lax.ppermute(x, "dp", [(i, target(i) % devices) for i in range(devices)])


def far_of(i):
    return i + REACH if i % 2 else i - REACH


def first_own(prompts, me, branches):
    own = jnp.int32(branches - 1)
    for slot in reversed(range(branches)):
        own = jnp.where(prompts[slot] == me, slot, own)
    return own


def other_branch(step, prompts, me, branches):
    own = first_own(prompts, me, branches)
    return step + jnp.where(step >= own, 1, 0)


def source_of(prompt, me, devices):
    rel = lax.rem(prompt - me + devices, devices)
    rel = jnp.where(rel > REACH, rel - devices, rel)
    odd = lax.rem(me, 2) == 1
    source = jnp.where(rel == 0, OWN, FAR)
    source = jnp.where(rel == -2, LOW, source)
    source = jnp.where(rel == 2, HIGH, source)
    source = jnp.where(rel == 1, jnp.where(odd, HIGH_PAIR, PARTNER), source)
    source = jnp.where(rel == -1, jnp.where(odd, PARTNER, LOW_PAIR), source)
    source = jnp.where(rel == 3, jnp.where(odd, FAR, HIGH_PAIR), source)
    source = jnp.where(rel == -3, jnp.where(odd, LOW_PAIR, FAR), source)
    return source


def contract(a, b, dim_a, dim_b):
    return lax.dot_general(
        a, b, (((dim_a,), (dim_b,)), ((), ())), preferred_element_type=jnp.float32
    )


def split_pairs(pairs, wide):
    rows = pairs.shape[0] // 2
    wide[...] = pairs.astype(jnp.float32)
    return [wide[pl.ds(at, rows, stride=2), :].astype(jnp.bfloat16) for at in range(2)]


def load_split(chunk, pairs, wide, split):
    size = wide.shape[1]
    keys, values = split_pairs(pairs[chunk * size : (chunk + 1) * size, :], wide.at[chunk % 2])
    split[chunk % 2, :, :HD] = keys
    split[chunk % 2, :, HD:] = values


def project_kernel(prefix_ref, weight_ref, out_ref, rows, pairs, wide, split, sems):
    depth = rows.shape[1] // CHUNKS
    copies = []
    for chunk in range(CHUNKS):
        deep = pl.ds(chunk * depth, depth)
        both = pl.ds(chunk * 2 * depth, 2 * depth)
        copies.append(
            (
                pltpu.make_async_copy(weight_ref.at[both, :], pairs.at[both, :], sems.at[0, chunk]),
                pltpu.make_async_copy(prefix_ref.at[:, deep], rows.at[:, deep], sems.at[1, chunk]),
            )
        )
    for pair in copies:
        for copy in pair:
            copy.start()
    total = jnp.zeros((rows.shape[0], out_ref.shape[1]), jnp.float32)
    for chunk in range(CHUNKS + 1):
        if chunk < CHUNKS:
            for copy in copies[chunk]:
                copy.wait()
            load_split(chunk, pairs, wide, split)
        if chunk:
            part = rows[:, (chunk - 1) * depth : chunk * depth]
            total += contract(part, split[(chunk - 1) % 2], 1, 0)
    out_ref[...] = total.astype(out_ref.dtype)


def project(prefix, kv_weight):
    prefix_len, model_width = prefix.shape
    there = pl.BlockSpec(memory_space=pl.ANY)
    return pl.pallas_call(
        project_kernel,
        in_specs=[there] * 2,
        out_specs=pl.BlockSpec(memory_space=pltpu.VMEM),
        out_shape=jax.ShapeDtypeStruct((prefix_len, 2 * HD), jnp.bfloat16),
        scratch_shapes=[
            pltpu.VMEM(prefix.shape, jnp.bfloat16),
            pltpu.VMEM((2 * model_width, HD), jnp.bfloat16),
            pltpu.VMEM((2, 2 * model_width // CHUNKS, HD), jnp.float32),
            pltpu.VMEM((2, model_width // CHUNKS, 2 * HD), jnp.bfloat16),
            pltpu.SemaphoreType.DMA((2, CHUNKS)),
        ],
        compiler_params=pltpu.CompilerParams(vmem_limit_bytes=PROJECT_VMEM),
        cost_estimate=pl.CostEstimate(
            flops=4 * prefix_len * model_width * HD,
            bytes_accessed=2 * model_width * (prefix_len + 2 * HD),
            transcendentals=0,
        ),
        name="project",
    )(prefix, kv_weight.reshape(2 * model_width, HD))


def back_kernel(part, index, *refs):
    *grads, weight_ref, far_give, far_keep, near_give, near_keep, wide, split = refs
    depth = split.shape[1]
    chunks = far_give.shape[1] // depth
    rows = far_give.shape[0]
    half, side = index[0] >> 1, index[0] & 1
    owners = (
        2 * (1 - half) + 1 - side,
        2 * (1 - half) + side,
        2 * half + 1 - side,
        2 * half + side,
    )
    parts = []
    for owner in owners:
        at = pl.ds(pl.multiple_of(owner * rows, rows), rows)
        total = grads[0][at, :].astype(jnp.float32)
        for grad in grads[1:]:
            total = total + grad[at, :].astype(jnp.float32)
        parts.append(total.astype(jnp.bfloat16))
    kv_grad = jnp.concatenate(parts, axis=0)
    for chunk in range(chunks + 1):
        if chunk < chunks:
            load_split(part * chunks + chunk, weight_ref, wide, split)
        if chunk:
            share = contract(kv_grad, split[(part * chunks + chunk - 1) % 2], 1, 1).astype(jnp.bfloat16)
            cols = pl.ds((chunk - 1) * depth, depth)
            for number, out in enumerate((far_give, far_keep, near_give, near_keep)):
                out[:, cols] = share[number * rows : (number + 1) * rows]


def back_shares(index, grads, kv_weight, count, part):
    model_width = kv_weight.shape[0]
    rows = grads[0].shape[0] // count
    here = pl.BlockSpec(memory_space=pltpu.VMEM)
    return pl.pallas_call(
        functools.partial(back_kernel, part),
        in_specs=[pl.BlockSpec(memory_space=pltpu.SMEM)]
        + [here] * (len(grads) + 1),
        out_specs=[here] * 4,
        out_shape=[jax.ShapeDtypeStruct((rows, model_width // PARTS), jnp.bfloat16)] * 4,
        scratch_shapes=[
            pltpu.VMEM((2, 2 * model_width // CHUNKS, HD), jnp.float32),
            pltpu.VMEM((2, model_width // CHUNKS, 2 * HD), jnp.bfloat16),
        ],
        compiler_params=pltpu.CompilerParams(vmem_limit_bytes=VMEM),
        cost_estimate=pl.CostEstimate(
            flops=4 * grads[0].shape[0] * model_width * HD // PARTS,
            bytes_accessed=2 * model_width * (grads[0].shape[0] + 2 * HD) // PARTS,
            transcendentals=0,
        ),
        name="back_shares",
    )(index, *grads, kv_weight.reshape(2 * model_width, HD))


def head_pass(heads, base, q_ref, up_ref, out_ref, keys, values, scratch, prefix_len):
    answers = keys.shape[0] - prefix_len
    scale = HD**-0.5 * math.log2(math.e)
    units = [(at, block) for at in range(0, len(heads), TALL) for block in range(answers // ROWS)]
    scores_at, probs_at, lead_at, half_grad, half_prob = scratch
    tall_rows = min(TALL, len(heads)) * ROWS

    def place(unit):
        at, block = units[unit]
        mine = range(at, min(at + TALL, len(heads)))
        return mine, block * ROWS, prefix_len + (block + 1) * ROWS

    def tall(ref, unit):
        mine, start, _ = place(unit)
        rows = pl.ds(pl.multiple_of(base + start, ROWS), ROWS)
        return jnp.concatenate(
            [ref[rows, heads[at] * HD : (heads[at] + 1) * HD] for at in mine], axis=0
        )

    def score(unit):
        seen = place(unit)[2]
        scores_at[unit % 2, :, :seen] = contract(tall(q_ref, unit), keys[:seen, :], 1, 1)

    def soften(unit):
        slot = unit % 2
        seen = place(unit)[2]
        for tile in range(tall_rows // TILE):
            rows = pl.ds(tile * TILE, TILE)
            first = tile * TILE % ROWS
            edge = seen - ROWS + first // BLOCK * BLOCK
            scores = scores_at[slot, rows, : edge + BLOCK]
            rows_at = lax.broadcasted_iota(jnp.int32, (TILE, BLOCK), 0) + first % BLOCK
            keys_at = lax.broadcasted_iota(jnp.int32, (TILE, BLOCK), 1)
            last = jnp.where(keys_at <= rows_at, scores[:, edge:], -jnp.inf)
            scores = jnp.concatenate([scores[:, :edge], last], axis=1)
            row_max = jnp.max(scores, axis=1, keepdims=True)
            exps = jnp.exp2((scores - row_max) * scale)
            probs = exps * (1.0 / jnp.sum(exps, axis=1, keepdims=True))
            lead_at[slot, rows, :] = probs[:, :prefix_len]
            probs_at[slot, rows, : edge + BLOCK] = probs.astype(jnp.bfloat16)
            if edge + BLOCK < seen:
                probs_at[slot, rows, edge + BLOCK : seen] = jnp.zeros(
                    (TILE, seen - edge - BLOCK), jnp.bfloat16
                )

    def finish(unit):
        slot = unit % 2
        mine, start, seen = place(unit)
        context = contract(probs_at[slot, :, :seen], values[:seen, :], 1, 0)
        upstream = tall(up_ref, unit)
        prob_grad = contract(upstream, values[:prefix_len, :], 1, 1)
        for number, head in enumerate(mine):
            out_ref[start : start + ROWS, head * HD : (head + 1) * HD] = context[
                number * ROWS : (number + 1) * ROWS
            ].astype(jnp.bfloat16)
        delta_row = jnp.sum(upstream.astype(jnp.float32) * context, axis=1, keepdims=True)
        score_grad = lead_at[slot] * (prob_grad - delta_row)
        at = pl.ds(unit * tall_rows, tall_rows)
        half_grad[at, :] = score_grad.astype(jnp.bfloat16)
        half_prob[at, :] = probs_at[slot, :, :prefix_len]

    score(0)
    for unit in range(len(units)):
        if unit + 1 < len(units):
            score(unit + 1)
        soften(unit)
        if unit:
            finish(unit - 1)
    finish(len(units) - 1)

    def gathered(ref):
        return jnp.concatenate([tall(ref, unit) for unit in range(len(units))], axis=0)

    key_grad = contract(half_grad[...], gathered(q_ref), 0, 0)
    value_grad = contract(half_prob[...], gathered(up_ref), 0, 0)
    return jnp.concatenate([key_grad * HD**-0.5, value_grad], axis=1)


def fill(keys, values, piece, kv_ref, base, wide):
    size = wide.shape[0]
    prefix_len = keys.shape[0] - size // 2
    keys[:prefix_len, :] = piece[:, :HD]
    values[:prefix_len, :] = piece[:, HD:]
    pairs = kv_ref[pl.ds(pl.multiple_of(2 * base, size), size), :]
    keys[prefix_len:, :], values[prefix_len:, :] = split_pairs(pairs, wide)


def branch_pass(heads, base, source, pieces, q_ref, kv_ref, up_ref, out_ref, buffers):
    wide, keys, values, *scratch = buffers
    prefix_len = keys.shape[0] - wide.shape[0] // 2
    if len(pieces) == 1:
        fill(keys, values, pieces[0], kv_ref, base, wide)
    else:
        for number, piece in enumerate(pieces):

            @pl.when(source == number)
            def _(piece=piece):
                fill(keys, values, piece, kv_ref, base, wide)

    return head_pass(heads, base, q_ref, up_ref, out_ref, keys, values, scratch, prefix_len)


def own_kernel(heads, answers, branches, later, info, prompts, own_ref, q_ref, kv_ref, up_ref, *refs):
    out_ref, own_grad, *buffers = refs[1:] if later else refs
    base = first_own(prompts, info[0], branches) * answers
    own_grad[...] = branch_pass(
        heads, base, None, [own_ref], q_ref, kv_ref, up_ref, out_ref, buffers
    )


def other_kernel(heads, answers, branches, devices, info, prompts, *refs):
    pieces = refs[:SOURCES]
    q_ref, kv_ref, up_ref, _, out_ref, own_grad, far_grad, grad_ref = refs[SOURCES : SOURCES + 8]
    *buffers, own_total, far_total = refs[SOURCES + 8 :]
    step = pl.program_id(0)
    me = info[0]
    branch = other_branch(step, prompts, me, branches)
    source = source_of(prompts[branch], me, devices)
    grad = branch_pass(
        heads, branch * answers, source, pieces, q_ref, kv_ref, up_ref, out_ref, buffers
    )
    own_part = jnp.where(source == OWN, grad, 0.0)
    far_part = jnp.where(source == FAR, grad, 0.0)
    prefix_len = grad.shape[0]
    grad_ref[step, :prefix_len, :] = grad.astype(jnp.bfloat16)
    prompt = prompts[branch].astype(jnp.float32)
    grad_ref[step, prefix_len:, :] = jnp.full((NOTES, grad.shape[1]), prompt).astype(jnp.bfloat16)

    @pl.when(step == 0)
    def _():
        own_total[...] = own_part
        far_total[...] = far_part

    @pl.when(step > 0)
    def _():
        own_total[...] += own_part
        far_total[...] += far_part

    @pl.when(step == pl.num_programs(0) - 1)
    def _():
        own_grad[...] = own_total[...]
        far_grad[...] = far_total[...].astype(jnp.bfloat16)


def relay_kernel(branches, devices, info, prompts, grad_ref, got_ref, *outs):
    to_low, to_high, to_me = outs
    me = info[0]
    down, up = lax.rem(me + devices - 2, devices), lax.rem(me + 2, devices)
    low = high = kept = jnp.zeros(to_me.shape, jnp.float32)
    prefix_len = to_me.shape[0]
    for number in range(branches - 1):
        grad = grad_ref[number, :prefix_len, :].astype(jnp.float32)
        prompt = prompts[other_branch(number, prompts, me, branches)]
        low = low + jnp.where(prompt == down, grad, 0.0)
        high = high + jnp.where(prompt == up, grad, 0.0)
        grad = got_ref[number, :prefix_len, :].astype(jnp.float32)
        prompt = got_ref[number, prefix_len : prefix_len + NOTES, :].astype(jnp.float32)[:1]
        low = low + jnp.where(prompt == down.astype(jnp.float32), grad, 0.0)
        high = high + jnp.where(prompt == up.astype(jnp.float32), grad, 0.0)
        kept = kept + jnp.where(prompt == me.astype(jnp.float32), grad, 0.0)
    to_low[...] = low.astype(jnp.bfloat16)
    to_high[...] = high.astype(jnp.bfloat16)
    to_me[...] = kept


def relay(devices, me, prompts, grad, got):
    branches = prompts.shape[0]
    here = pl.BlockSpec(memory_space=pltpu.VMEM)
    shape = (grad.shape[1] - NOTES, grad.shape[2])
    return pl.pallas_call(
        functools.partial(relay_kernel, branches, devices),
        grid_spec=pltpu.PrefetchScalarGridSpec(
            num_scalar_prefetch=2, grid=(1,), in_specs=[here] * 2, out_specs=[here] * 3
        ),
        out_shape=[
            jax.ShapeDtypeStruct(shape, jnp.bfloat16),
            jax.ShapeDtypeStruct(shape, jnp.bfloat16),
            jax.ShapeDtypeStruct(shape, jnp.float32),
        ],
        compiler_params=pltpu.CompilerParams(vmem_limit_bytes=VMEM),
        name="relay",
    )(me, prompts, grad, got)


def attention(own, heads, devices, me, prompts, pieces, query, pairs, upstream, out):
    branches = prompts.shape[0]
    answers = query.shape[0] // branches
    prefix_len = pieces[0].shape[0]
    width = len(heads) * HD
    steps = 1 if own else branches - 1

    def out_at(step, info, prompts):
        if own:
            return first_own(prompts, info[0], branches), heads[0] // len(heads)
        return other_branch(step, prompts, info[0], branches), 0

    here = pl.BlockSpec(memory_space=pltpu.VMEM)
    there = pl.BlockSpec(memory_space=pl.ANY)
    piece = (prefix_len, 2 * HD)
    operands = [*pieces, query, pairs, upstream]
    in_specs = [here] * len(operands)
    out_shape = [
        jax.ShapeDtypeStruct(query.shape, query.dtype),
        jax.ShapeDtypeStruct(piece, jnp.float32),
    ]
    out_specs = [pl.BlockSpec((answers, width), out_at), here]
    aliases = {}
    if out is not None:
        aliases = {2 + len(operands): 0}
        operands.append(out)
        in_specs.append(there)
    tall_rows = min(TALL, len(heads)) * ROWS
    all_rows = len(heads) * answers
    scratch = [
        pltpu.VMEM((2 * answers, HD), jnp.float32),
        pltpu.VMEM((prefix_len + answers, HD), jnp.bfloat16),
        pltpu.VMEM((prefix_len + answers, HD), jnp.bfloat16),
        pltpu.VMEM((2, tall_rows, prefix_len + answers), jnp.float32),
        pltpu.VMEM((2, tall_rows, prefix_len + answers), jnp.bfloat16),
        pltpu.VMEM((2, tall_rows, prefix_len), jnp.float32),
        pltpu.VMEM((all_rows, prefix_len), jnp.bfloat16),
        pltpu.VMEM((all_rows, prefix_len), jnp.bfloat16),
    ]
    if own:
        body = functools.partial(own_kernel, heads, answers, branches, out is not None)
    else:
        body = functools.partial(other_kernel, heads, answers, branches, devices)
        scratch += [pltpu.VMEM(piece, jnp.float32)] * 2
        for shape in (piece, (steps, prefix_len + NOTES, 2 * HD)):
            out_shape.append(jax.ShapeDtypeStruct(shape, jnp.bfloat16))
            out_specs.append(here)
    seen = prefix_len + (answers + BLOCK) // 2
    work = steps * answers * width
    return pl.pallas_call(
        body,
        grid_spec=pltpu.PrefetchScalarGridSpec(
            num_scalar_prefetch=2,
            grid=(steps,),
            in_specs=in_specs,
            out_specs=out_specs,
            scratch_shapes=scratch,
        ),
        out_shape=out_shape,
        input_output_aliases=aliases,
        compiler_params=pltpu.CompilerParams(
            dimension_semantics=("arbitrary",), vmem_limit_bytes=VMEM
        ),
        cost_estimate=pl.CostEstimate(
            flops=work * (4 * seen + 6 * prefix_len),
            bytes_accessed=6 * work,
            transcendentals=work // HD * seen,
        ),
        name="own_branch" if own else "other_branches",
    )(me, prompts, *operands)


def shards(prefix, kv_weight, ans_query, ans_kv, d_out, branch_prompt):
    columns = kv_weight.shape[2]
    if columns != HD:
        raise ValueError("one kv head")
    devices = lax.axis_size("dp")
    if devices % 2 or devices < 2 * REACH + 1:
        raise ValueError("dp size")
    if devices > 256:
        raise ValueError("notes size")
    me = lax.axis_index("dp").astype(jnp.int32).reshape(1)
    answer_pairs = ans_kv.reshape(2 * ans_kv.shape[0], HD)
    own_kv = project(prefix[0], kv_weight)
    partner = dp_permute(own_kv, lambda i: i ^ 1)
    far = dp_permute(own_kv, far_of)
    low = dp_permute(own_kv, lambda i: i + 2)
    high = dp_permute(own_kv, lambda i: i - 2)
    low_pair = dp_permute(partner, lambda i: i + 2)
    high_pair = dp_permute(partner, lambda i: i - 2)
    branch = functools.partial(
        attention,
        devices=devices,
        me=me,
        prompts=branch_prompt,
        query=ans_query,
        pairs=answer_pairs,
        upstream=d_out,
    )
    heads = tuple(range(ans_query.shape[1] // HD))
    early, late = heads[: len(heads) // 2], heads[len(heads) // 2 :]
    out, early_grad = branch(own=True, heads=early, pieces=[own_kv], out=None)
    out, more_grad, to_far, grad = branch(
        own=False, heads=heads, pieces=[own_kv, partner, low, low_pair, high, high_pair, far], out=out
    )
    from_far = dp_permute(to_far, far_of)
    got = dp_permute(grad, lambda i: i ^ 1)
    out, late_grad = branch(own=True, heads=late, pieces=[own_kv], out=out)
    to_low, to_high, to_me = relay(devices, me, branch_prompt, grad, got)
    from_high = dp_permute(to_low, lambda i: i - 2)
    from_low = dp_permute(to_high, lambda i: i + 2)
    grads = [early_grad, late_grad, more_grad, to_me, from_far, from_high, from_low]
    rows = project_back(grads, kv_weight)
    return (out, rows.reshape(1, *rows.shape))


def project_back(grads, kv_weight):
    count = lax.axis_size("tensor")
    if count != 4:
        raise ValueError("tensor size")
    index = lax.axis_index("tensor").astype(jnp.int32).reshape(1)

    def swap(x, bit):
        return lax.ppermute(x, "tensor", [(i, i ^ bit) for i in range(count)])

    def both(a, b):
        return (a.astype(jnp.float32) + b.astype(jnp.float32)).astype(jnp.bfloat16)

    shares = [back_shares(index, grads, kv_weight, count, part) for part in range(PARTS)]
    arrived, mine = [], []
    for far_give, far_keep, _, _ in shares:
        got = swap(far_give, 1)
        arrived.append(swap(both(far_keep, got), 2))
    for _, _, near_give, near_keep in shares:
        got = swap(near_give, 1)
        mine.append(lax.optimization_barrier(both(near_keep, got)))
    return jnp.concatenate([both(a, b) for a, b in zip(mine, arrived)], axis=1)


def solution(mesh):
    return jax.shard_map(
        shards,
        mesh=mesh,
        in_specs=(
            P("dp", None, None),
            P(None, None, "tensor"),
            P("dp", "tensor"),
            P("dp", None, "tensor"),
            P("dp", "tensor"),
            P("dp"),
        ),
        out_specs=(P("dp", "tensor"), P("dp", "tensor", None)),
        check_vma=False,
    )
```

```python
import functools
import math

import jax
import jax.numpy as jnp
from jax import lax
from jax.experimental import pallas as pl
from jax.experimental.pallas import tpu as pltpu
from jax.sharding import PartitionSpec as P

HD = 128
REACH = 3
BLOCK = 128
ROWS = 128
TALL = 4
TILE = 32
CHUNKS = 8
BACK_CHUNKS = 2
VMEM = 24 << 20
PARTS = 2
PROJECT_VMEM = 54500000
NOTES = 16
OWN, PARTNER, LOW, LOW_PAIR, HIGH, HIGH_PAIR, FAR, SOURCES = range(8)


def dp_permute(x, target):
    devices = lax.axis_size("dp")
    return lax.ppermute(x, "dp", [(i, target(i) % devices) for i in range(devices)])


def far_of(i):
    return i + REACH if i % 2 else i - REACH


def first_own(prompts, me, branches):
    own = jnp.int32(branches - 1)
    for slot in reversed(range(branches)):
        own = jnp.where(prompts[slot] == me, slot, own)
    return own


def other_branch(step, prompts, me, branches):
    own = first_own(prompts, me, branches)
    return step + jnp.where(step >= own, 1, 0)


def source_of(prompt, me, devices):
    rel = lax.rem(prompt - me + devices, devices)
    rel = jnp.where(rel > REACH, rel - devices, rel)
    odd = lax.rem(me, 2) == 1
    source = jnp.where(rel == 0, OWN, FAR)
    source = jnp.where(rel == -2, LOW, source)
    source = jnp.where(rel == 2, HIGH, source)
    source = jnp.where(rel == 1, jnp.where(odd, HIGH_PAIR, PARTNER), source)
    source = jnp.where(rel == -1, jnp.where(odd, PARTNER, LOW_PAIR), source)
    source = jnp.where(rel == 3, jnp.where(odd, FAR, HIGH_PAIR), source)
    source = jnp.where(rel == -3, jnp.where(odd, LOW_PAIR, FAR), source)
    return source


def contract(a, b, dim_a, dim_b):
    return lax.dot_general(
        a, b, (((dim_a,), (dim_b,)), ((), ())), preferred_element_type=jnp.float32
    )


def split_pairs(pairs, wide):
    rows = pairs.shape[0] // 2
    wide[...] = pairs.astype(jnp.float32)
    return [wide[pl.ds(at, rows, stride=2), :].astype(jnp.bfloat16) for at in range(2)]


def load_split(chunk, pairs, wide, split):
    size = wide.shape[1]
    keys, values = split_pairs(pairs[chunk * size : (chunk + 1) * size, :], wide.at[chunk % 2])
    split[chunk % 2, :, :HD] = keys
    split[chunk % 2, :, HD:] = values


def project_kernel(prefix_ref, weight_ref, out_ref, rows, pairs, wide, split, sems):
    depth = rows.shape[1] // CHUNKS
    copies = []
    for chunk in range(CHUNKS):
        deep = pl.ds(chunk * depth, depth)
        both = pl.ds(chunk * 2 * depth, 2 * depth)
        copies.append(
            (
                pltpu.make_async_copy(weight_ref.at[both, :], pairs.at[both, :], sems.at[0, chunk]),
                pltpu.make_async_copy(prefix_ref.at[:, deep], rows.at[:, deep], sems.at[1, chunk]),
            )
        )
    for pair in copies:
        for copy in pair:
            copy.start()
    total = jnp.zeros((rows.shape[0], out_ref.shape[1]), jnp.float32)
    for chunk in range(CHUNKS + 1):
        if chunk < CHUNKS:
            for copy in copies[chunk]:
                copy.wait()
            load_split(chunk, pairs, wide, split)
        if chunk:
            part = rows[:, (chunk - 1) * depth : chunk * depth]
            total += contract(part, split[(chunk - 1) % 2], 1, 0)
    out_ref[...] = total.astype(out_ref.dtype)


def project(prefix, kv_weight):
    prefix_len, model_width = prefix.shape
    there = pl.BlockSpec(memory_space=pl.ANY)
    return pl.pallas_call(
        project_kernel,
        in_specs=[there] * 2,
        out_specs=pl.BlockSpec(memory_space=pltpu.VMEM),
        out_shape=jax.ShapeDtypeStruct((prefix_len, 2 * HD), jnp.bfloat16),
        scratch_shapes=[
            pltpu.VMEM(prefix.shape, jnp.bfloat16),
            pltpu.VMEM((2 * model_width, HD), jnp.bfloat16),
            pltpu.VMEM((2, 2 * model_width // CHUNKS, HD), jnp.float32),
            pltpu.VMEM((2, model_width // CHUNKS, 2 * HD), jnp.bfloat16),
            pltpu.SemaphoreType.DMA((2, CHUNKS)),
        ],
        compiler_params=pltpu.CompilerParams(vmem_limit_bytes=PROJECT_VMEM),
        cost_estimate=pl.CostEstimate(
            flops=4 * prefix_len * model_width * HD,
            bytes_accessed=2 * model_width * (prefix_len + 2 * HD),
            transcendentals=0,
        ),
        name="project",
    )(prefix, kv_weight.reshape(2 * model_width, HD))


def back_kernel(part, index, *refs):
    *grads, weight_ref, far_give, far_keep, near_give, near_keep, wide, split = refs
    depth = split.shape[1]
    chunks = far_give.shape[1] // depth
    rows = far_give.shape[0]
    half, side = index[0] >> 1, index[0] & 1
    owners = (
        2 * (1 - half) + 1 - side,
        2 * (1 - half) + side,
        2 * half + 1 - side,
        2 * half + side,
    )
    parts = []
    for owner in owners:
        at = pl.ds(pl.multiple_of(owner * rows, rows), rows)
        total = grads[0][at, :].astype(jnp.float32)
        for grad in grads[1:]:
            total = total + grad[at, :].astype(jnp.float32)
        parts.append(total.astype(jnp.bfloat16))
    kv_grad = jnp.concatenate(parts, axis=0)
    for chunk in range(chunks + 1):
        if chunk < chunks:
            load_split(part * chunks + chunk, weight_ref, wide, split)
        if chunk:
            share = contract(kv_grad, split[(part * chunks + chunk - 1) % 2], 1, 1).astype(jnp.bfloat16)
            cols = pl.ds((chunk - 1) * depth, depth)
            for number, out in enumerate((far_give, far_keep, near_give, near_keep)):
                out[:, cols] = share[number * rows : (number + 1) * rows]


def back_shares(index, grads, kv_weight, count, part):
    model_width = kv_weight.shape[0]
    rows = grads[0].shape[0] // count
    here = pl.BlockSpec(memory_space=pltpu.VMEM)
    return pl.pallas_call(
        functools.partial(back_kernel, part),
        in_specs=[pl.BlockSpec(memory_space=pltpu.SMEM)]
        + [here] * (len(grads) + 1),
        out_specs=[here] * 4,
        out_shape=[jax.ShapeDtypeStruct((rows, model_width // PARTS), jnp.bfloat16)] * 4,
        scratch_shapes=[
            pltpu.VMEM((2, 2 * model_width // BACK_CHUNKS, HD), jnp.float32),
            pltpu.VMEM((2, model_width // BACK_CHUNKS, 2 * HD), jnp.bfloat16),
        ],
        compiler_params=pltpu.CompilerParams(vmem_limit_bytes=VMEM),
        cost_estimate=pl.CostEstimate(
            flops=4 * grads[0].shape[0] * model_width * HD // PARTS,
            bytes_accessed=2 * model_width * (grads[0].shape[0] + 2 * HD) // PARTS,
            transcendentals=0,
        ),
        name="back_shares",
    )(index, *grads, kv_weight.reshape(2 * model_width, HD))


def head_pass(heads, base, q_ref, up_ref, out_ref, keys, values, scratch, prefix_len):
    answers = keys.shape[0] - prefix_len
    scale = HD**-0.5 * math.log2(math.e)
    units = [(at, block) for at in range(0, len(heads), TALL) for block in range(answers // ROWS)]
    scores_at, probs_at, lead_at, half_grad, half_prob = scratch
    tall_rows = min(TALL, len(heads)) * ROWS

    def place(unit):
        at, block = units[unit]
        mine = range(at, min(at + TALL, len(heads)))
        return mine, block * ROWS, prefix_len + (block + 1) * ROWS

    def tall(ref, unit):
        mine, start, _ = place(unit)
        rows = pl.ds(pl.multiple_of(base + start, ROWS), ROWS)
        return jnp.concatenate(
            [ref[rows, heads[at] * HD : (heads[at] + 1) * HD] for at in mine], axis=0
        )

    def score(unit):
        seen = place(unit)[2]
        scores_at[unit % 2, :, :seen] = contract(tall(q_ref, unit), keys[:seen, :], 1, 1)

    def soften(unit):
        slot = unit % 2
        seen = place(unit)[2]
        for tile in range(tall_rows // TILE):
            rows = pl.ds(tile * TILE, TILE)
            first = tile * TILE % ROWS
            edge = seen - ROWS + first // BLOCK * BLOCK
            scores = scores_at[slot, rows, : edge + BLOCK]
            rows_at = lax.broadcasted_iota(jnp.int32, (TILE, BLOCK), 0) + first % BLOCK
            keys_at = lax.broadcasted_iota(jnp.int32, (TILE, BLOCK), 1)
            last = jnp.where(keys_at <= rows_at, scores[:, edge:], -jnp.inf)
            scores = jnp.concatenate([scores[:, :edge], last], axis=1)
            row_max = jnp.max(scores, axis=1, keepdims=True)
            exps = jnp.exp2((scores - row_max) * scale)
            probs = exps * (1.0 / jnp.sum(exps, axis=1, keepdims=True))
            lead_at[slot, rows, :] = probs[:, :prefix_len]
            probs_at[slot, rows, : edge + BLOCK] = probs.astype(jnp.bfloat16)
            if edge + BLOCK < seen:
                probs_at[slot, rows, edge + BLOCK : seen] = jnp.zeros(
                    (TILE, seen - edge - BLOCK), jnp.bfloat16
                )

    def finish(unit):
        slot = unit % 2
        mine, start, seen = place(unit)
        context = contract(probs_at[slot, :, :seen], values[:seen, :], 1, 0)
        upstream = tall(up_ref, unit)
        prob_grad = contract(upstream, values[:prefix_len, :], 1, 1)
        for number, head in enumerate(mine):
            out_ref[start : start + ROWS, head * HD : (head + 1) * HD] = context[
                number * ROWS : (number + 1) * ROWS
            ].astype(jnp.bfloat16)
        delta_row = jnp.sum(upstream.astype(jnp.float32) * context, axis=1, keepdims=True)
        score_grad = lead_at[slot] * (prob_grad - delta_row)
        at = pl.ds(unit * tall_rows, tall_rows)
        half_grad[at, :] = score_grad.astype(jnp.bfloat16)
        half_prob[at, :] = probs_at[slot, :, :prefix_len]

    score(0)
    for unit in range(len(units)):
        if unit + 1 < len(units):
            score(unit + 1)
        soften(unit)
        if unit:
            finish(unit - 1)
    finish(len(units) - 1)

    def gathered(ref):
        return jnp.concatenate([tall(ref, unit) for unit in range(len(units))], axis=0)

    key_grad = contract(half_grad[...], gathered(q_ref), 0, 0)
    value_grad = contract(half_prob[...], gathered(up_ref), 0, 0)
    return jnp.concatenate([key_grad * HD**-0.5, value_grad], axis=1)


def fill(keys, values, piece, kv_ref, base, wide):
    size = wide.shape[0]
    prefix_len = keys.shape[0] - size // 2
    keys[:prefix_len, :] = piece[:, :HD]
    values[:prefix_len, :] = piece[:, HD:]
    pairs = kv_ref[pl.ds(pl.multiple_of(2 * base, size), size), :]
    keys[prefix_len:, :], values[prefix_len:, :] = split_pairs(pairs, wide)


def branch_pass(heads, base, source, pieces, q_ref, kv_ref, up_ref, out_ref, buffers):
    wide, keys, values, *scratch = buffers
    prefix_len = keys.shape[0] - wide.shape[0] // 2
    if len(pieces) == 1:
        fill(keys, values, pieces[0], kv_ref, base, wide)
    else:
        for number, piece in enumerate(pieces):

            @pl.when(source == number)
            def _(piece=piece):
                fill(keys, values, piece, kv_ref, base, wide)

    return head_pass(heads, base, q_ref, up_ref, out_ref, keys, values, scratch, prefix_len)


def own_kernel(heads, answers, branches, later, info, prompts, own_ref, q_ref, kv_ref, up_ref, *refs):
    out_ref, own_grad, *buffers = refs[1:] if later else refs
    base = first_own(prompts, info[0], branches) * answers
    own_grad[...] = branch_pass(
        heads, base, None, [own_ref], q_ref, kv_ref, up_ref, out_ref, buffers
    )


def other_kernel(heads, answers, branches, devices, info, prompts, *refs):
    pieces = refs[:SOURCES]
    q_ref, kv_ref, up_ref, _, out_ref, own_grad, far_grad, grad_ref = refs[SOURCES : SOURCES + 8]
    *buffers, own_total, far_total = refs[SOURCES + 8 :]
    step = pl.program_id(0)
    me = info[0]
    branch = other_branch(step, prompts, me, branches)
    source = source_of(prompts[branch], me, devices)
    grad = branch_pass(
        heads, branch * answers, source, pieces, q_ref, kv_ref, up_ref, out_ref, buffers
    )
    own_part = jnp.where(source == OWN, grad, 0.0)
    far_part = jnp.where(source == FAR, grad, 0.0)
    prefix_len = grad.shape[0]
    grad_ref[step, :prefix_len, :] = grad.astype(jnp.bfloat16)
    prompt = prompts[branch].astype(jnp.float32)
    grad_ref[step, prefix_len:, :] = jnp.full((NOTES, grad.shape[1]), prompt).astype(jnp.bfloat16)

    @pl.when(step == 0)
    def _():
        own_total[...] = own_part
        far_total[...] = far_part

    @pl.when(step > 0)
    def _():
        own_total[...] += own_part
        far_total[...] += far_part

    @pl.when(step == pl.num_programs(0) - 1)
    def _():
        own_grad[...] = own_total[...]
        far_grad[...] = far_total[...].astype(jnp.bfloat16)


def relay_kernel(branches, devices, info, prompts, grad_ref, got_ref, *outs):
    to_low, to_high, to_me = outs
    me = info[0]
    down, up = lax.rem(me + devices - 2, devices), lax.rem(me + 2, devices)
    low = high = kept = jnp.zeros(to_me.shape, jnp.float32)
    prefix_len = to_me.shape[0]
    for number in range(branches - 1):
        grad = grad_ref[number, :prefix_len, :].astype(jnp.float32)
        prompt = prompts[other_branch(number, prompts, me, branches)]
        low = low + jnp.where(prompt == down, grad, 0.0)
        high = high + jnp.where(prompt == up, grad, 0.0)
        grad = got_ref[number, :prefix_len, :].astype(jnp.float32)
        prompt = got_ref[number, prefix_len : prefix_len + NOTES, :].astype(jnp.float32)[:1]
        low = low + jnp.where(prompt == down.astype(jnp.float32), grad, 0.0)
        high = high + jnp.where(prompt == up.astype(jnp.float32), grad, 0.0)
        kept = kept + jnp.where(prompt == me.astype(jnp.float32), grad, 0.0)
    to_low[...] = low.astype(jnp.bfloat16)
    to_high[...] = high.astype(jnp.bfloat16)
    to_me[...] = kept


def relay(devices, me, prompts, grad, got):
    branches = prompts.shape[0]
    here = pl.BlockSpec(memory_space=pltpu.VMEM)
    shape = (grad.shape[1] - NOTES, grad.shape[2])
    return pl.pallas_call(
        functools.partial(relay_kernel, branches, devices),
        grid_spec=pltpu.PrefetchScalarGridSpec(
            num_scalar_prefetch=2, grid=(1,), in_specs=[here] * 2, out_specs=[here] * 3
        ),
        out_shape=[
            jax.ShapeDtypeStruct(shape, jnp.bfloat16),
            jax.ShapeDtypeStruct(shape, jnp.bfloat16),
            jax.ShapeDtypeStruct(shape, jnp.float32),
        ],
        compiler_params=pltpu.CompilerParams(vmem_limit_bytes=VMEM),
        name="relay",
    )(me, prompts, grad, got)


def attention(own, heads, devices, me, prompts, pieces, query, pairs, upstream, out):
    branches = prompts.shape[0]
    answers = query.shape[0] // branches
    prefix_len = pieces[0].shape[0]
    width = len(heads) * HD
    steps = 1 if own else branches - 1

    def out_at(step, info, prompts):
        if own:
            return first_own(prompts, info[0], branches), heads[0] // len(heads)
        return other_branch(step, prompts, info[0], branches), 0

    here = pl.BlockSpec(memory_space=pltpu.VMEM)
    there = pl.BlockSpec(memory_space=pl.ANY)
    piece = (prefix_len, 2 * HD)
    operands = [*pieces, query, pairs, upstream]
    in_specs = [here] * len(operands)
    out_shape = [
        jax.ShapeDtypeStruct(query.shape, query.dtype),
        jax.ShapeDtypeStruct(piece, jnp.float32),
    ]
    out_specs = [pl.BlockSpec((answers, width), out_at), here]
    aliases = {}
    if out is not None:
        aliases = {2 + len(operands): 0}
        operands.append(out)
        in_specs.append(there)
    tall_rows = min(TALL, len(heads)) * ROWS
    all_rows = len(heads) * answers
    scratch = [
        pltpu.VMEM((2 * answers, HD), jnp.float32),
        pltpu.VMEM((prefix_len + answers, HD), jnp.bfloat16),
        pltpu.VMEM((prefix_len + answers, HD), jnp.bfloat16),
        pltpu.VMEM((2, tall_rows, prefix_len + answers), jnp.float32),
        pltpu.VMEM((2, tall_rows, prefix_len + answers), jnp.bfloat16),
        pltpu.VMEM((2, tall_rows, prefix_len), jnp.float32),
        pltpu.VMEM((all_rows, prefix_len), jnp.bfloat16),
        pltpu.VMEM((all_rows, prefix_len), jnp.bfloat16),
    ]
    if own:
        body = functools.partial(own_kernel, heads, answers, branches, out is not None)
    else:
        body = functools.partial(other_kernel, heads, answers, branches, devices)
        scratch += [pltpu.VMEM(piece, jnp.float32)] * 2
        for shape in (piece, (steps, prefix_len + NOTES, 2 * HD)):
            out_shape.append(jax.ShapeDtypeStruct(shape, jnp.bfloat16))
            out_specs.append(here)
    seen = prefix_len + (answers + BLOCK) // 2
    work = steps * answers * width
    return pl.pallas_call(
        body,
        grid_spec=pltpu.PrefetchScalarGridSpec(
            num_scalar_prefetch=2,
            grid=(steps,),
            in_specs=in_specs,
            out_specs=out_specs,
            scratch_shapes=scratch,
        ),
        out_shape=out_shape,
        input_output_aliases=aliases,
        compiler_params=pltpu.CompilerParams(
            dimension_semantics=("arbitrary",), vmem_limit_bytes=VMEM
        ),
        cost_estimate=pl.CostEstimate(
            flops=work * (4 * seen + 6 * prefix_len),
            bytes_accessed=6 * work,
            transcendentals=work // HD * seen,
        ),
        name="own_branch" if own else "other_branches",
    )(me, prompts, *operands)


def shards(prefix, kv_weight, ans_query, ans_kv, d_out, branch_prompt):
    columns = kv_weight.shape[2]
    if columns != HD:
        raise ValueError("one kv head")
    devices = lax.axis_size("dp")
    if devices % 2 or devices < 2 * REACH + 1:
        raise ValueError("dp size")
    if devices > 256:
        raise ValueError("notes size")
    me = lax.axis_index("dp").astype(jnp.int32).reshape(1)
    answer_pairs = ans_kv.reshape(2 * ans_kv.shape[0], HD)
    own_kv = project(prefix[0], kv_weight)
    partner = dp_permute(own_kv, lambda i: i ^ 1)
    far = dp_permute(own_kv, far_of)
    low = dp_permute(own_kv, lambda i: i + 2)
    high = dp_permute(own_kv, lambda i: i - 2)
    low_pair = dp_permute(partner, lambda i: i + 2)
    high_pair = dp_permute(partner, lambda i: i - 2)
    branch = functools.partial(
        attention,
        devices=devices,
        me=me,
        prompts=branch_prompt,
        query=ans_query,
        pairs=answer_pairs,
        upstream=d_out,
    )
    heads = tuple(range(ans_query.shape[1] // HD))
    early, late = heads[: len(heads) // 2], heads[len(heads) // 2 :]
    out, early_grad = branch(own=True, heads=early, pieces=[own_kv], out=None)
    out, more_grad, to_far, grad = branch(
        own=False, heads=heads, pieces=[own_kv, partner, low, low_pair, high, high_pair, far], out=out
    )
    from_far = dp_permute(to_far, far_of)
    got = dp_permute(grad, lambda i: i ^ 1)
    out, late_grad = branch(own=True, heads=late, pieces=[own_kv], out=out)
    to_low, to_high, to_me = relay(devices, me, branch_prompt, grad, got)
    from_high = dp_permute(to_low, lambda i: i - 2)
    from_low = dp_permute(to_high, lambda i: i + 2)
    grads = [early_grad, late_grad, more_grad, to_me, from_far, from_high, from_low]
    rows = project_back(grads, kv_weight)
    return (out, rows.reshape(1, *rows.shape))


def project_back(grads, kv_weight):
    count = lax.axis_size("tensor")
    if count != 4:
        raise ValueError("tensor size")
    index = lax.axis_index("tensor").astype(jnp.int32).reshape(1)

    def swap(x, bit):
        return lax.ppermute(x, "tensor", [(i, i ^ bit) for i in range(count)])

    def both(a, b):
        return (a.astype(jnp.float32) + b.astype(jnp.float32)).astype(jnp.bfloat16)

    shares = [back_shares(index, grads, kv_weight, count, part) for part in range(PARTS)]
    arrived, mine = [], []
    for far_give, far_keep, _, _ in shares:
        got = swap(far_give, 1)
        arrived.append(swap(both(far_keep, got), 2))
    for _, _, near_give, near_keep in shares:
        got = swap(near_give, 1)
        mine.append(lax.optimization_barrier(both(near_keep, got)))
    return jnp.concatenate([both(a, b) for a, b in zip(mine, arrived)], axis=1)


def solution(mesh):
    return jax.shard_map(
        shards,
        mesh=mesh,
        in_specs=(
            P("dp", None, None),
            P(None, None, "tensor"),
            P("dp", "tensor"),
            P("dp", None, "tensor"),
            P("dp", "tensor"),
            P("dp"),
        ),
        out_specs=(P("dp", "tensor"), P("dp", "tensor", None)),
        check_vma=False,
    )
```
